512 devices in a mesh: utt: 8 (over x, core), tm: 64 (over y, z).
Axes of the slice: x: 4, y: 8, z: 8, core: 2. Of those that a mesh axis runs over, the one named last changes fastest.
Arguments:
- phone_ids: int32 [8, 4096], P('utt', 'tm'), may hold values from 0 to 255
- durations: int32 [8, 4096], P('utt'), may hold values from 1 to 16, 16384 in all within a row
- utt_lengths: int32 [8, 64], P('utt'), may hold values from 1 to 256, 4096 in all within a row
- utt_order: int32 [8, 64], P('utt'), may hold values from 0 to 63, each once within a row
- buckets: int32 [8, 64, 8], P('utt', 'tm'), may hold values from 0 to 7, each once within a row
- embed_table: bfloat16 [256, 384], replicated, may hold values from -6 to 6
- conv1_weight: bfloat16 [3456, 768], P(None, 'tm'), may hold values from -0.109375 to 0.109375
- conv2_weight: bfloat16 [384, 768], P(None, 'tm'), may hold values from -0.21875 to 0.21875
- norm_gain: float32 [384], replicated, may hold values from 0.1 to 1.9
- mel_weight: bfloat16 [384, 80], replicated, may hold values from -0.3125 to 0.3125
- pre_weight: bfloat16 [7, 80, 512], replicated, may hold values from -0.25 to 0.25
- up_weight: bfloat16 [512, 16, 256], P('tm'), may hold values from -0.1875 to 0.1875
Outputs:
- bucketed: bfloat16 [8, 64, 8, 256, 256], P('utt', 'tm')
The draws below stay inside these ranges and needn't reach their ends.
All inputs are finite; a program needn't handle non-finite values.
Results may differ from the reference program's by a relative error of at most 0.0067.
Values may be sent and summed in bfloat16 or wider, within the bound.
A program may use at most 64 MiB of HBM per device.

```python
import math
import jax
import jax.numpy as jnp
import numpy as np
from jax import lax

D = 384
FILT = 768
KP = 9
VOCAB = 256
MEL = 80
CH = 512
CHO = 256
MAXDUR = 16
NU = 64
P_DEV = 64
F_DEV = 256
PH_GRP = 4096
FR_GRP = 16384
ULMOST = 256
PIECE = 256
N_UTT = 8
N_TM = 64


def place_ends(result, rng, low, top_value):
    longest = result.shape.index(max(result.shape))
    spots = []
    for shift in (0, 1):
        where = [jax.random.randint(jax.random.fold_in(rng, axis), (), 0, length) for axis, length in enumerate(result.shape)]
        where[longest] = (where[longest] + shift) % result.shape[longest]
        spots.append(tuple(where))
    return result.at[spots[0]].set(low).at[spots[1]].set(top_value)


def block_levels(stream_key, dims, split, low, largest):
    def one(position, blocks):
        heights = jax.random.uniform(jax.random.fold_in(jax.random.fold_in(stream_key, 6), position), (blocks,), jnp.float32, low / len(split), largest / len(split))
        return jnp.repeat(jnp.exp(heights), dims[position] // blocks).reshape((-1,) + (1,) * (len(dims) - position - 1))

    gain = one(*split[0])
    for cut in split[1:]:
        gain = gain * one(*cut)
    return gain


def profile(number_of, total, limit, skew):
    weights = [(1 << 20) // math.isqrt(standing ** skew) + 1 for standing in range(2, number_of + 1)]
    surplus, given = total - limit - (number_of - 1), [1] * (number_of - 1)
    while surplus > 0:
        candidates = [i for i in range(number_of - 1) if given[i] < limit]
        pool, remaining = sum([weights[i] for i in candidates]), surplus
        for i in candidates:
            more = min(limit - given[i], max(1, remaining * weights[i] // pool), surplus)
            given[i] = given[i] + more
            surplus = surplus - more
    return np.array([limit] + given)


def ragged_sizes(key, number_of, total, reach, lean):
    if number_of == 2:
        one = jax.random.randint(key, (), max(1, total - reach), min(reach, total - 1) + 1)
        return jnp.stack([one, total - one])
    tallies = jnp.asarray(profile(number_of, total, reach, lean), jnp.int32)
    pairs = (number_of - 1) // 2
    giver, taker = tallies[1:1 + 2 * pairs:2], tallies[2:2 + 2 * pairs:2]
    margin = jnp.minimum(giver - 1, reach - taker)
    passed = jax.random.randint(jax.random.fold_in(key, 1), (pairs,), 0, 1 << 20) % (margin + 1)
    tallies = tallies.at[1:1 + 2 * pairs:2].set(giver - passed).at[2:2 + 2 * pairs:2].set(taker + passed)
    return tallies[jax.random.permutation(jax.random.fold_in(key, 2), number_of)]


def bell_draw(stream_key, dims, scale, bound, pieces=(), kind=jnp.bfloat16):
    result = jax.random.normal(stream_key, dims, jnp.float32) * scale
    if len(pieces) > 0:
        result = block_levels(stream_key, dims, pieces, -0.22, 0.18) * result
    return jnp.clip(result, min=-bound, max=bound).astype(kind)


def setup_inputs(seed: int = 0) -> dict:
    keys = jax.random.split(jax.random.key(seed), 13)
    return {
        "phone_ids": place_ends(jax.random.randint(keys[0], (N_UTT, PH_GRP), 0, VOCAB), jax.random.fold_in(keys[0], 1), 0, VOCAB - 1).astype(jnp.int32),
        "durations": jax.vmap(lambda own: ragged_sizes(own, PH_GRP, F_DEV * N_TM, MAXDUR, 2))(jax.random.split(keys[1], N_UTT)).reshape((N_UTT, PH_GRP)).astype(jnp.int32),
        "utt_lengths": jax.vmap(lambda own: ragged_sizes(own, NU, P_DEV * N_TM, ULMOST, 2))(jax.random.split(keys[2], N_UTT)).reshape((N_UTT, NU)).astype(jnp.int32),
        "utt_order": jax.vmap(lambda own: jax.random.permutation(own, NU))(jax.random.split(keys[3], N_UTT)).reshape((N_UTT, NU)).astype(jnp.int32),
        "buckets": jax.vmap(lambda own: jax.random.permutation(own, N_UTT))(jax.random.split(keys[4], N_UTT * N_TM)).reshape((N_UTT, N_TM, N_UTT)).astype(jnp.int32),
        "embed_table": bell_draw(keys[5], (VOCAB, D), 1.0, 6.0),
        "conv1_weight": bell_draw(keys[6], (KP * D, FILT), (KP * D) ** -0.5, 0.109375, ((1, 64),)),
        "conv2_weight": bell_draw(keys[7], (D, FILT), FILT ** -0.5, 0.21875, ((1, 64),)),
        "norm_gain": jnp.clip(1.0 + 0.18 * jax.random.normal(keys[8], (D,), jnp.float32), 0.1, 1.9),
        "mel_weight": bell_draw(keys[9], (D, MEL), D ** -0.5, 0.3125),
        "pre_weight": bell_draw(keys[10], (7, MEL, CH), (7 * MEL) ** -0.5, 0.25),
        "up_weight": bell_draw(keys[11], (CH, 16, CHO), (2 * CH) ** -0.5, 0.1875, ((0, 64),)),
    }


EPS = 1e-05

def utterance_of(indices, bounds):
    return lax.optimization_barrier(jnp.sum((bounds[None, :] <= indices[:, None]).astype(jnp.int32), axis=1)).astype(jnp.int32)

def frame_layout(lasting, lengths, ordering):
    phone_index = jnp.arange(PH_GRP, dtype=jnp.int32)
    bounds = jnp.cumsum(lengths).astype(jnp.int32)
    utt_first = (bounds - lengths).astype(jnp.int32)
    owners = utterance_of(phone_index, bounds)
    inclusive = jnp.cumsum(lasting).astype(jnp.int32)
    exclusive = (inclusive - lasting).astype(jnp.int32)
    first_frame = jnp.take(exclusive, utt_first)
    utt_frames = jnp.take(inclusive, bounds - 1) - first_frame
    slots = jnp.arange(NU, dtype=jnp.int32)
    places = lax.optimization_barrier(jnp.sum(jnp.where(ordering[None, :] == slots[:, None], slots[None, :], 0), axis=1)).astype(jnp.int32)
    offsets = lax.optimization_barrier(jnp.sum(jnp.where(places[None, :] < places[:, None], utt_frames[None, :], 0), axis=1)).astype(jnp.int32)
    starting = (jnp.take(offsets, owners) + exclusive - jnp.take(first_frame, owners)).astype(jnp.int32)
    return (starting, owners)

def synth_group(phones, lasting, lengths, ordering, embed_table, conv1_weight, conv2_weight, norm_gain, mel_weight, pre_weight, up_weight):
    starting, owners = frame_layout(lasting, lengths, ordering)
    embedded = jnp.take(embed_table, phones, axis=0)
    padded = jnp.pad(embedded, ((4, 4), (0, 0)))
    labels = jnp.pad(owners, 4, constant_values=-1)
    running = jnp.zeros((PH_GRP, FILT), jnp.float32)
    for tap in range(KP):
        keep = (labels[tap:tap + PH_GRP] == owners)[:, None]
        running = running + jnp.dot(jnp.where(keep, padded[tap:tap + PH_GRP], 0), conv1_weight[tap * D:(tap + 1) * D], preferred_element_type=jnp.float32)
    filters = jnp.maximum(running, 0.0).astype(jnp.bfloat16)
    resid = embedded.astype(jnp.float32) + jnp.dot(filters, conv2_weight.T, preferred_element_type=jnp.float32)
    center = lax.optimization_barrier(jnp.mean(resid, axis=1, keepdims=True))
    spread = lax.optimization_barrier(jnp.mean((resid - center) ** 2, axis=1, keepdims=True))
    decoded = ((resid - center) * lax.rsqrt(spread + EPS) * norm_gain[None, :]).astype(jnp.bfloat16)
    mel_ph = jnp.dot(decoded, mel_weight, preferred_element_type=jnp.float32).astype(jnp.bfloat16)
    sorting = jnp.argsort(starting).astype(jnp.int32)
    sorted_start = jnp.take(starting, sorting)
    frame_index = jnp.arange(FR_GRP, dtype=jnp.int32)
    located = (jnp.searchsorted(sorted_start, frame_index, side='right') - 1).astype(jnp.int32)
    phone_of = jnp.take(sorting, located)
    mel_frames = jnp.take(mel_ph, phone_of, axis=0)
    frame_utt = jnp.take(owners, phone_of)
    mel_pad = jnp.pad(mel_frames, ((3, 3), (0, 0)))
    frame_labels = jnp.pad(frame_utt, 3, constant_values=-1)
    summed = jnp.zeros((FR_GRP, CH), jnp.float32)
    for tap in range(7):
        keep = (frame_labels[tap:tap + FR_GRP] == frame_utt)[:, None]
        summed = summed + jnp.dot(jnp.where(keep, mel_pad[tap:tap + FR_GRP], 0), pre_weight[tap], preferred_element_type=jnp.float32)
    act = jnp.where(summed >= 0, summed, 0.1 * summed).astype(jnp.bfloat16)
    middle = jnp.dot(act, up_weight[:, 4:12, :].reshape(CH, 8 * CHO), preferred_element_type=jnp.float32)
    zero_row = jnp.zeros((1, CH), jnp.bfloat16)
    act_prev = jnp.concatenate([zero_row, act[:-1]], axis=0)
    act_next = jnp.concatenate([act[1:], zero_row], axis=0)
    same_prev = jnp.concatenate([jnp.zeros((1,), bool), frame_utt[1:] == frame_utt[:-1]])
    same_next = jnp.concatenate([frame_utt[:-1] == frame_utt[1:], jnp.zeros((1,), bool)])
    before = jnp.dot(jnp.where(same_prev[:, None], act_prev, 0), up_weight[:, 12:16, :].reshape(CH, 4 * CHO), preferred_element_type=jnp.float32)
    after = jnp.dot(jnp.where(same_next[:, None], act_next, 0), up_weight[:, 0:4, :].reshape(CH, 4 * CHO), preferred_element_type=jnp.float32)
    joined = middle + jnp.concatenate([before, after], axis=1)
    return joined.astype(jnp.bfloat16).reshape(FR_GRP * 8, CHO)

def reference(phone_ids, durations, utt_lengths, utt_order, buckets, embed_table, conv1_weight, conv2_weight, norm_gain, mel_weight, pre_weight, up_weight):
    results = []
    for group in range(N_UTT):
        results.append(synth_group(phone_ids[group], durations[group], utt_lengths[group], utt_order[group], embed_table, conv1_weight, conv2_weight, norm_gain, mel_weight, pre_weight, up_weight))
    waves = jnp.stack(results).reshape(N_UTT, N_TM, N_UTT, PIECE, CHO)
    slots = jnp.arange(N_UTT, dtype=jnp.int32)
    inverse = lax.optimization_barrier(jnp.sum(jnp.where(buckets[:, :, :, None] == slots[None, None, None, :], slots[None, None, :, None], 0), axis=2)).astype(jnp.int32)
    picked = jnp.take_along_axis(waves, inverse[:, :, :, None, None], axis=2)
    return jnp.transpose(picked, (2, 1, 0, 3, 4))
```

```python
import functools

import jax
import jax.numpy as jnp
from jax import lax
from jax.experimental import pallas as pl
from jax.experimental.pallas import tpu as pltpu
from jax.sharding import PartitionSpec as P

F_DEV = 256
SIDE = 8
WIDE = 128
REACH = 4
EPS = 1e-05
MESH = pl.DeviceIdType.MESH
BF = jnp.bfloat16


def gather_kernel(count, share, *refs):
    blocks = refs[:count]
    outs = refs[count : 2 * count]
    local_sem, first_send, first_recv, ring_send, ring_recv, pair_send, pair_recv = refs[2 * count :]
    utt = lax.axis_index("utt")
    tm = lax.axis_index("tm")
    core = lax.rem(utt, 2)
    pair = utt + 1 - 2 * core
    y = lax.div(tm, SIDE)
    z = lax.rem(tm, SIDE)
    first = y + core * (z - y)
    second = z + core * (y - z)
    half = core if share else 0

    def place(a, b):
        return a * SIDE + b + core * ((b - a) * SIDE + (a - b))

    barrier = pltpu.get_barrier_semaphore()

    def greet(step, carry):
        pl.semaphore_signal(
            barrier, inc=1,
            device_id=(utt, place(lax.rem(first + step, SIDE), second)), device_id_type=MESH,
        )
        return carry

    lax.fori_loop(1, SIDE, greet, 0)
    up = lax.rem(second + 1, SIDE)
    down = lax.rem(second + SIDE - 1, SIDE)
    for side in (up, down):
        pl.semaphore_signal(barrier, inc=1, device_id=(utt, place(first, side)), device_id_type=MESH)
    if share:
        pl.semaphore_signal(barrier, inc=1, device_id=(pair, tm), device_id_type=MESH)
    pl.semaphore_wait(barrier, SIDE + 1 + (1 if share else 0))

    own = [
        pltpu.make_async_copy(blocks[i], outs[i].at[half, second, first], local_sem.at[i])
        for i in range(count)
    ]
    for copy in own:
        copy.start()

    def first_copy(i, step):
        return pltpu.make_async_remote_copy(
            src_ref=blocks[i],
            dst_ref=outs[i].at[half, second, first],
            send_sem=first_send.at[i, step],
            recv_sem=first_recv.at[i, step],
            device_id=(utt, place(lax.rem(first + step, SIDE), second)),
            device_id_type=MESH,
        )

    for i in range(count):
        for step in range(1, SIDE):
            first_copy(i, step).start()
    for copy in own:
        copy.wait()
    for i in range(count):
        for step in range(1, SIDE):
            first_copy(i, step).wait_recv()

    def ring_copy(i, way, step):
        slot = lax.rem(second - step + SIDE, SIDE) if way == 0 else lax.rem(second + step, SIDE)
        row = outs[i].at[half, slot]
        return pltpu.make_async_remote_copy(
            src_ref=row,
            dst_ref=row,
            send_sem=ring_send.at[i, way, step],
            recv_sem=ring_recv.at[i, way, step],
            device_id=(utt, place(first, up if way == 0 else down)),
            device_id_type=MESH,
        )

    def pair_copy(i, slot, number):
        row = outs[i].at[half, slot]
        return pltpu.make_async_remote_copy(
            src_ref=row,
            dst_ref=row,
            send_sem=pair_send.at[i, number],
            recv_sem=pair_recv.at[i, number],
            device_id=(pair, tm),
            device_id_type=MESH,
        )

    pairs = []

    def hand_over(i, slot, number):
        if share:
            copy = pair_copy(i, slot, number)
            copy.start()
            pairs.append(copy)

    ways = ((0, SIDE // 2), (1, SIDE // 2 - 1))
    for i in range(count):
        for way, _ in ways:
            ring_copy(i, way, 0).start()
        hand_over(i, second, 0)
    for step in range(SIDE // 2):
        for i in range(count):
            for way, steps in ways:
                if step < steps:
                    ring_copy(i, way, step).wait_recv()
                    if step + 1 < steps:
                        ring_copy(i, way, step + 1).start()
                    if way == 0:
                        slot = lax.rem(second - step - 1 + SIDE, SIDE)
                    else:
                        slot = lax.rem(second + step + 1, SIDE)
                    hand_over(i, slot, 1 + 2 * step + way)
    for copy in pairs:
        copy.wait_recv()
    for i in range(count):
        for step in range(1, SIDE):
            first_copy(i, step).wait_send()
        for way, steps in ways:
            for step in range(steps):
                ring_copy(i, way, step).wait_send()
    for copy in pairs:
        copy.wait_send()


def gather_blocks(blocks, share, number):
    count = len(blocks)
    halves = 2 if share else 1
    return pl.pallas_call(
        functools.partial(gather_kernel, count, share),
        out_shape=[
            jax.ShapeDtypeStruct((halves, SIDE, SIDE) + block.shape, block.dtype) for block in blocks
        ],
        in_specs=[pl.BlockSpec(memory_space=pl.ANY)] * count,
        out_specs=[pl.BlockSpec(memory_space=pl.ANY)] * count,
        scratch_shapes=[
            pltpu.SemaphoreType.DMA((count,)),
            pltpu.SemaphoreType.DMA((count, SIDE)),
            pltpu.SemaphoreType.DMA((count, SIDE)),
            pltpu.SemaphoreType.DMA((count, 2, SIDE // 2)),
            pltpu.SemaphoreType.DMA((count, 2, SIDE // 2)),
            pltpu.SemaphoreType.DMA((count, SIDE)),
            pltpu.SemaphoreType.DMA((count, SIDE)),
        ],
        compiler_params=pltpu.CompilerParams(collective_id=number, has_side_effects=True),
        name=f"gather{number}",
    )(*blocks)


def utterance_of(indices, bounds):
    return jnp.sum((bounds[None, :] <= indices[:, None]).astype(jnp.int32), axis=1)


def frame_layout(lasting, lengths, ordering):
    phone_total = lasting.shape[0]
    utt_count = lengths.shape[0]
    phone_index = jnp.arange(phone_total, dtype=jnp.int32)
    bounds = jnp.cumsum(lengths)
    utt_first = bounds - lengths
    inclusive = jnp.cumsum(lasting)
    exclusive = inclusive - lasting
    first_frame = jnp.take(exclusive, utt_first)
    utt_frames = jnp.take(inclusive, bounds - 1) - first_frame
    slots = jnp.arange(utt_count, dtype=jnp.int32)
    places = jnp.sum(jnp.where(ordering[None, :] == slots[:, None], slots[None, :], 0), axis=1)
    offsets = jnp.sum(jnp.where(places[None, :] < places[:, None], utt_frames[None, :], 0), axis=1)
    moved = offsets - first_frame
    member = (bounds[None, :] > phone_index[:, None]) & (utt_first[None, :] <= phone_index[:, None])
    starting = exclusive + jnp.sum(jnp.where(member, moved[None, :], 0), axis=1)
    return (starting, bounds)


def shards(
    phone_ids,
    durations,
    utt_lengths,
    utt_order,
    buckets,
    embed_table,
    conv1_weight,
    conv2_weight,
    norm_gain,
    mel_weight,
    pre_weight,
    up_weight,
):
    phone_count = phone_ids.shape[1]
    width = embed_table.shape[1]
    device = lax.axis_index("tm")
    core = lax.rem(lax.axis_index("utt"), 2)
    ends = lax.axis_size("tm") - 1

    filters_here = conv1_weight.shape[1]
    part = filters_here // 2
    pad = ((0, 0), (0, 8 - part), (0, 0))
    inward = jnp.pad(conv1_weight.T.reshape(2, part, -1), pad)
    outward = jnp.pad(conv2_weight.T.reshape(2, part, -1), pad)
    rising = jnp.transpose(up_weight, (1, 0, 2)).reshape(2, 8, up_weight.shape[0], -1)
    pick = lambda both: jnp.where(core == 0, both[0], both[1])
    inward, outward, rising = gather_blocks([pick(inward), pick(outward), pick(rising)], True, 1)
    rows = 2 * SIDE * SIDE * 8
    inward = inward.reshape(rows, -1)
    outward = outward.reshape(rows, -1)

    starting, bounds = frame_layout(durations[0], utt_lengths[0], utt_order[0])
    ending = starting + durations[0]
    nearby = device * phone_count + jnp.arange(-4, phone_count + 4, dtype=jnp.int32)
    phone_labels = jnp.where(nearby < 0, -1, utterance_of(nearby, bounds))
    head = lax.ppermute(phone_ids[0, :4], "tm", [(i + 1, i) for i in range(ends)])
    tail = lax.ppermute(phone_ids[0, -4:], "tm", [(i, i + 1) for i in range(ends)])
    ids = jnp.concatenate([tail, phone_ids[0], head])
    symbols = embed_table.shape[0]
    choose = (ids[:, None] == jnp.arange(symbols, dtype=jnp.int32)[None, :]).astype(BF)
    widened = jnp.dot(choose, embed_table, preferred_element_type=jnp.float32).astype(BF)
    center = phone_labels[4 : 4 + phone_count]
    columns = []
    for tap in range(9):
        keep = (phone_labels[tap : tap + phone_count] == center)[:, None]
        columns.append(jnp.where(keep, widened[tap : tap + phone_count], jnp.zeros((), BF)))
    unfolded = jnp.concatenate(columns, axis=1)
    filters = jnp.maximum(
        lax.dot_general(
            unfolded, inward, (((1,), (1,)), ((), ())), preferred_element_type=jnp.float32
        ),
        0.0,
    ).astype(BF)
    conv_out = jnp.dot(filters, outward, preferred_element_type=jnp.float32)
    resid = widened[4 : 4 + phone_count].astype(jnp.float32) + conv_out
    middle = jnp.mean(resid, axis=1, keepdims=True)
    spread = jnp.mean((resid - middle) ** 2, axis=1, keepdims=True)
    decoded = ((resid - middle) * lax.rsqrt(spread + EPS) * norm_gain[None, :]).astype(BF)
    mel_width = mel_weight.shape[1]
    mel_ph = jnp.dot(decoded, mel_weight, preferred_element_type=jnp.float32).astype(BF)
    lane = lax.broadcasted_iota(jnp.int32, (phone_count, WIDE), 1)
    told = jnp.where(lane == mel_width, (center + 1).astype(BF)[:, None], jnp.zeros((), BF))
    mel_block = jnp.pad(mel_ph, ((0, 0), (0, WIDE - mel_width))) + told
    (portion,) = gather_blocks([mel_block], False, 2)
    portion = portion.reshape(-1, WIDE)

    def arranged(values):
        cells = values.reshape(SIDE, SIDE, phone_count)
        return jnp.where(core == 0, jnp.transpose(cells, (1, 0, 2)), cells).reshape(-1)

    groups = lax.axis_size("utt")
    piece = F_DEV // groups
    span = piece + 2 * REACH
    slots = jnp.arange(groups, dtype=jnp.int32)
    source = jnp.sum(
        jnp.where(buckets[0, 0][None, :] == slots[:, None], slots[None, :], 0), axis=1
    )
    frames = (
        device * F_DEV + source[:, None] * piece - REACH
        + jnp.arange(span, dtype=jnp.int32)[None, :]
    ).reshape(-1)
    hit = (frames[:, None] >= arranged(starting)[None, :]) & (
        frames[:, None] < arranged(ending)[None, :]
    )
    windows = jnp.dot(hit.astype(BF), portion, preferred_element_type=jnp.float32).astype(BF)
    arrived = lax.all_to_all(
        windows.reshape(groups, span, WIDE), "utt", split_axis=0, concat_axis=0, tiled=True
    )

    labels = arrived[:, :, mel_width]
    channels = pre_weight.shape[2]
    pre_flat = jnp.pad(pre_weight, ((0, 0), (0, WIDE - mel_width), (0, 0))).reshape(-1, channels)
    inner = piece + 2
    mine = labels[:, 3 : 3 + inner]
    columns = []
    for tap in range(7):
        keep = (labels[:, tap : tap + inner] == mine)[:, :, None]
        columns.append(jnp.where(keep, arrived[:, tap : tap + inner], jnp.zeros((), BF)))
    unfolded = jnp.concatenate(columns, axis=2).reshape(groups * inner, -1)
    summed = jnp.dot(unfolded, pre_flat, preferred_element_type=jnp.float32)
    act = jnp.where(summed >= 0, summed, 0.1 * summed).astype(BF).reshape(groups, inner, channels)
    now = act[:, 1 : 1 + piece].reshape(F_DEV, channels)
    keep_prev = (mine[:, :piece] == mine[:, 1 : 1 + piece])[:, :, None]
    keep_next = (mine[:, 2:] == mine[:, 1 : 1 + piece])[:, :, None]
    prev = jnp.where(keep_prev, act[:, :piece], jnp.zeros((), BF)).reshape(F_DEV, channels)
    nxt = jnp.where(keep_next, act[:, 2:], jnp.zeros((), BF)).reshape(F_DEV, channels)

    out_width = up_weight.shape[2]
    early = jnp.transpose(rising[0], (2, 1, 0, 3, 4))
    late = jnp.transpose(rising[1], (2, 0, 1, 3, 4))
    early = early.reshape(8, channels, out_width)
    late = late.reshape(8, channels, out_width)
    upsampled = upsample(now, prev, nxt, early, late)
    return upsampled.reshape(1, 1, groups, -1, out_width)


def upsample_kernel(now, prev, nxt, early, late, out, total):
    f32 = jnp.float32
    for r in range(8):
        if r < 4:
            value = jnp.dot(now[...], early[r + 4], preferred_element_type=f32)
            value += jnp.dot(prev[...], late[r + 4], preferred_element_type=f32)
        else:
            value = jnp.dot(now[...], late[r - 4], preferred_element_type=f32)
            value += jnp.dot(nxt[...], early[r - 4], preferred_element_type=f32)
        total[:, r, :] = value
    out[...] = total[...].astype(out.dtype)


def upsample(now, prev, nxt, early, late):
    frames, channels = now.shape
    width = early.shape[2]
    rows = 64
    tile = pl.BlockSpec((rows, channels), lambda i: (i, 0))
    whole = pl.BlockSpec((8, channels, width), lambda i: (0, 0, 0))
    return pl.pallas_call(
        upsample_kernel,
        grid=(frames // rows,),
        out_shape=jax.ShapeDtypeStruct((frames, 8, width), BF),
        in_specs=[tile, tile, tile, whole, whole],
        out_specs=pl.BlockSpec((rows, 8, width), lambda i: (i, 0, 0)),
        scratch_shapes=[pltpu.VMEM((rows, 8, width), jnp.float32)],
        name="upsample",
    )(now, prev, nxt, early, late)


def solution(mesh):
    placed = (
        P("utt", "tm"),
        P("utt", None),
        P("utt", None),
        P("utt", None),
        P("utt", "tm", None),
        P(),
        P(None, "tm"),
        P(None, "tm"),
        P(),
        P(),
        P(),
        P("tm", None, None),
    )
    return jax.shard_map(
        shards,
        mesh=mesh,
        in_specs=placed,
        out_specs=P("utt", "tm", None, None, None),
        check_vma=False,
    )
```

```python
import functools

import jax
import jax.numpy as jnp
from jax import lax
from jax.experimental import pallas as pl
from jax.experimental.pallas import tpu as pltpu
from jax.sharding import PartitionSpec as P

F_DEV = 256
SIDE = 8
WIDE = 128
REACH = 4
EPS = 1e-05
MESH = pl.DeviceIdType.MESH
BF = jnp.bfloat16


def gather_kernel(count, share, swap, *refs):
    blocks = refs[:count]
    outs = refs[count + swap : 2 * count + swap]
    scratch = refs[2 * (count + swap) :]
    local_sem, first_send, first_recv, ring_send, ring_recv, pair_send, pair_recv = scratch[:7]
    utt = lax.axis_index("utt")
    tm = lax.axis_index("tm")
    core = lax.rem(utt, 2)
    pair = utt + 1 - 2 * core
    y = lax.div(tm, SIDE)
    z = lax.rem(tm, SIDE)
    first = y + core * (z - y)
    second = z + core * (y - z)
    half = core if share else 0

    def place(a, b):
        return a * SIDE + b + core * ((b - a) * SIDE + (a - b))

    barrier = pltpu.get_barrier_semaphore()

    def greet(step, carry):
        pl.semaphore_signal(
            barrier, inc=1,
            device_id=(utt, place(lax.rem(first + step, SIDE), second)), device_id_type=MESH,
        )
        return carry

    lax.fori_loop(1, SIDE, greet, 0)
    up = lax.rem(second + 1, SIDE)
    down = lax.rem(second + SIDE - 1, SIDE)
    for side in (up, down):
        pl.semaphore_signal(barrier, inc=1, device_id=(utt, place(first, side)), device_id_type=MESH)
    if share or swap:
        pl.semaphore_signal(barrier, inc=1, device_id=(pair, tm), device_id_type=MESH)
    pl.semaphore_wait(barrier, SIDE + 1 + (1 if share or swap else 0))

    own = [
        pltpu.make_async_copy(blocks[i], outs[i].at[half, second, first], local_sem.at[i])
        for i in range(count)
    ]
    for copy in own:
        copy.start()

    def first_copy(i, step):
        return pltpu.make_async_remote_copy(
            src_ref=blocks[i],
            dst_ref=outs[i].at[half, second, first],
            send_sem=first_send.at[i, step],
            recv_sem=first_recv.at[i, step],
            device_id=(utt, place(lax.rem(first + step, SIDE), second)),
            device_id_type=MESH,
        )

    for i in range(count):
        for step in range(1, SIDE):
            first_copy(i, step).start()
    swaps = []
    if swap:
        given, taken = refs[count], refs[2 * count + 1]
        pieces = scratch[7].shape[0]
        length = given.shape[0] // pieces
        for number in range(pieces):
            rows = pl.ds(number * length, length)
            copy = pltpu.make_async_remote_copy(
                src_ref=given.at[rows],
                dst_ref=taken.at[rows],
                send_sem=scratch[7].at[number],
                recv_sem=scratch[8].at[number],
                device_id=(pair, tm),
                device_id_type=MESH,
            )
            copy.start()
            swaps.append(copy)
    for copy in own:
        copy.wait()
    for i in range(count):
        for step in range(1, SIDE):
            first_copy(i, step).wait_recv()

    def ring_copy(i, way, step):
        slot = lax.rem(second - step + SIDE, SIDE) if way == 0 else lax.rem(second + step, SIDE)
        row = outs[i].at[half, slot]
        return pltpu.make_async_remote_copy(
            src_ref=row,
            dst_ref=row,
            send_sem=ring_send.at[i, way, step],
            recv_sem=ring_recv.at[i, way, step],
            device_id=(utt, place(first, up if way == 0 else down)),
            device_id_type=MESH,
        )

    def pair_copy(i, slot, number):
        row = outs[i].at[half, slot]
        return pltpu.make_async_remote_copy(
            src_ref=row,
            dst_ref=row,
            send_sem=pair_send.at[i, number],
            recv_sem=pair_recv.at[i, number],
            device_id=(pair, tm),
            device_id_type=MESH,
        )

    pairs = []

    def hand_over(i, slot, number):
        if share:
            copy = pair_copy(i, slot, number)
            copy.start()
            pairs.append(copy)

    ways = ((0, SIDE // 2), (1, SIDE // 2 - 1))
    for i in range(count):
        for way, _ in ways:
            ring_copy(i, way, 0).start()
        hand_over(i, second, 0)
    for step in range(SIDE // 2):
        for i in range(count):
            for way, steps in ways:
                if step < steps:
                    ring_copy(i, way, step).wait_recv()
                    if step + 1 < steps:
                        ring_copy(i, way, step + 1).start()
                    if way == 0:
                        slot = lax.rem(second - step - 1 + SIDE, SIDE)
                    else:
                        slot = lax.rem(second + step + 1, SIDE)
                    hand_over(i, slot, 1 + 2 * step + way)
    for copy in pairs:
        copy.wait_recv()
    for i in range(count):
        for step in range(1, SIDE):
            first_copy(i, step).wait_send()
        for way, steps in ways:
            for step in range(steps):
                ring_copy(i, way, step).wait_send()
    for copy in pairs:
        copy.wait_send()
    for copy in swaps:
        copy.wait()


def gather_blocks(blocks, share, number, space, swapped=None):
    count = len(blocks)
    halves = 2 if share else 1
    swap = 0 if swapped is None else 1
    scratch = [
        pltpu.SemaphoreType.DMA((count,)),
        pltpu.SemaphoreType.DMA((count, SIDE)),
        pltpu.SemaphoreType.DMA((count, SIDE)),
        pltpu.SemaphoreType.DMA((count, 2, SIDE // 2)),
        pltpu.SemaphoreType.DMA((count, 2, SIDE // 2)),
        pltpu.SemaphoreType.DMA((count, SIDE)),
        pltpu.SemaphoreType.DMA((count, SIDE)),
    ]
    shapes = [
        jax.ShapeDtypeStruct((halves, SIDE, SIDE) + block.shape, block.dtype) for block in blocks
    ]
    operands = list(blocks)
    if swap:
        scratch += [pltpu.SemaphoreType.DMA((4,)), pltpu.SemaphoreType.DMA((4,))]
        shapes.append(jax.ShapeDtypeStruct(swapped.shape, swapped.dtype))
        operands.append(swapped)
    specs = [pl.BlockSpec(memory_space=space)] * count
    specs += [pl.BlockSpec(memory_space=pl.ANY)] * swap
    return pl.pallas_call(
        functools.partial(gather_kernel, count, share, swap),
        out_shape=shapes,
        in_specs=specs,
        out_specs=specs,
        scratch_shapes=scratch,
        compiler_params=pltpu.CompilerParams(collective_id=number, has_side_effects=True),
        cost_estimate=pl.CostEstimate(flops=0, bytes_accessed=100_000_000, transcendentals=0),
        name=f"gather{number}",
    )(*operands)


def utterance_of(indices, bounds):
    return jnp.sum((bounds[None, :] <= indices[:, None]).astype(jnp.int32), axis=1)


def frame_layout(lasting, lengths, ordering):
    phone_total = lasting.shape[0]
    utt_count = lengths.shape[0]
    phone_index = jnp.arange(phone_total, dtype=jnp.int32)
    bounds = jnp.cumsum(lengths)
    utt_first = bounds - lengths
    inclusive = jnp.cumsum(lasting)
    exclusive = inclusive - lasting
    first_frame = jnp.take(exclusive, utt_first)
    utt_frames = jnp.take(inclusive, bounds - 1) - first_frame
    slots = jnp.arange(utt_count, dtype=jnp.int32)
    places = jnp.sum(jnp.where(ordering[None, :] == slots[:, None], slots[None, :], 0), axis=1)
    offsets = jnp.sum(jnp.where(places[None, :] < places[:, None], utt_frames[None, :], 0), axis=1)
    moved = offsets - first_frame
    member = (bounds[None, :] > phone_index[:, None]) & (utt_first[None, :] <= phone_index[:, None])
    starting = exclusive + jnp.sum(jnp.where(member, moved[None, :], 0), axis=1)
    return (starting, bounds)


def shards(
    phone_ids,
    durations,
    utt_lengths,
    utt_order,
    buckets,
    embed_table,
    conv1_weight,
    conv2_weight,
    norm_gain,
    mel_weight,
    pre_weight,
    up_weight,
):
    phone_count = phone_ids.shape[1]
    width = embed_table.shape[1]
    device = lax.axis_index("tm")
    core = lax.rem(lax.axis_index("utt"), 2)
    ends = lax.axis_size("tm") - 1

    symbols = embed_table.shape[0]
    filters_here = conv1_weight.shape[1]
    part = filters_here // 2
    pick = lambda both: jnp.where(core == 0, both[0], both[1])
    rising = pick(jnp.transpose(up_weight, (1, 0, 2)).reshape(2, 8, up_weight.shape[0], -1))
    own_taps = lax.all_gather(rising, "tm", axis=1, tiled=True)
    inward = pick(conv1_weight.T.reshape(2, part, -1)).reshape(part * 9, width)
    inward = lax.dot_general(
        inward, embed_table, (((1,), (1,)), ((), ())), preferred_element_type=jnp.float32
    ).astype(BF)
    inward = jnp.pad(inward.reshape(part, 9 * symbols), ((0, 8 - part), (0, 0)))
    outward = jnp.pad(pick(conv2_weight.T.reshape(2, part, -1)), ((0, 8 - part), (0, 0)))
    inward, outward = gather_blocks([inward, outward], True, 1, pl.ANY)
    rows = 2 * SIDE * SIDE * 8
    inward = inward.reshape(rows, -1)
    outward = outward.reshape(rows, -1)

    starting, bounds = frame_layout(durations[0], utt_lengths[0], utt_order[0])
    ending = starting + durations[0]
    nearby = device * phone_count + jnp.arange(-4, phone_count + 4, dtype=jnp.int32)
    phone_labels = jnp.where(nearby < 0, -1, utterance_of(nearby, bounds))
    head = lax.ppermute(phone_ids[0, :4], "tm", [(i + 1, i) for i in range(ends)])
    tail = lax.ppermute(phone_ids[0, -4:], "tm", [(i, i + 1) for i in range(ends)])
    ids = jnp.concatenate([tail, phone_ids[0], head])
    table = jnp.arange(symbols, dtype=jnp.int32)[None, :]
    chosen = (phone_ids[0][:, None] == table).astype(BF)
    embedded = jnp.dot(chosen, embed_table, preferred_element_type=jnp.float32)
    center = phone_labels[4 : 4 + phone_count]
    columns = []
    for tap in range(9):
        keep = phone_labels[tap : tap + phone_count] == center
        columns.append((jnp.where(keep, ids[tap : tap + phone_count], -1)[:, None] == table).astype(BF))
    unfolded = jnp.concatenate(columns, axis=1)
    filters = jnp.maximum(
        lax.dot_general(
            unfolded, inward, (((1,), (1,)), ((), ())), preferred_element_type=jnp.float32
        ),
        0.0,
    ).astype(BF)
    conv_out = jnp.dot(filters, outward, preferred_element_type=jnp.float32)
    resid = embedded + conv_out
    middle = jnp.mean(resid, axis=1, keepdims=True)
    spread = jnp.mean((resid - middle) ** 2, axis=1, keepdims=True)
    decoded = ((resid - middle) * lax.rsqrt(spread + EPS) * norm_gain[None, :]).astype(BF)
    mel_width = mel_weight.shape[1]
    mel_ph = jnp.dot(decoded, mel_weight, preferred_element_type=jnp.float32).astype(BF)
    lane = lax.broadcasted_iota(jnp.int32, (phone_count, WIDE), 1)
    told = jnp.where(lane == mel_width, (center + 1).astype(BF)[:, None], jnp.zeros((), BF))
    mel_block = jnp.pad(mel_ph, ((0, 0), (0, WIDE - mel_width))) + told
    portion, other_taps = gather_blocks([mel_block], False, 2, pltpu.VMEM, own_taps)
    portion = portion.reshape(-1, WIDE)

    def arranged(values):
        cells = values.reshape(SIDE, SIDE, phone_count)
        return jnp.where(core == 0, jnp.transpose(cells, (1, 0, 2)), cells).reshape(-1)

    groups = lax.axis_size("utt")
    piece = F_DEV // groups
    span = piece + 2 * REACH
    slots = jnp.arange(groups, dtype=jnp.int32)
    source = jnp.sum(
        jnp.where(buckets[0, 0][None, :] == slots[:, None], slots[None, :], 0), axis=1
    )
    frames = (
        device * F_DEV + source[:, None] * piece - REACH
        + jnp.arange(span, dtype=jnp.int32)[None, :]
    ).reshape(-1)
    hit = (frames[:, None] >= arranged(starting)[None, :]) & (
        frames[:, None] < arranged(ending)[None, :]
    )
    windows = jnp.dot(hit.astype(BF), portion, preferred_element_type=jnp.float32).astype(BF)
    arrived = lax.all_to_all(
        windows.reshape(groups, span, WIDE), "utt", split_axis=0, concat_axis=0, tiled=True
    )

    labels = arrived[:, :, mel_width]
    channels = pre_weight.shape[2]
    pre_flat = jnp.pad(pre_weight, ((0, 0), (0, WIDE - mel_width), (0, 0))).reshape(-1, channels)
    inner = piece + 2
    mine = labels[:, 3 : 3 + inner]
    columns = []
    for tap in range(7):
        keep = (labels[:, tap : tap + inner] == mine)[:, :, None]
        columns.append(jnp.where(keep, arrived[:, tap : tap + inner], jnp.zeros((), BF)))
    unfolded = jnp.concatenate(columns, axis=2).reshape(groups * inner, -1)
    summed = jnp.dot(unfolded, pre_flat, preferred_element_type=jnp.float32)
    act = jnp.where(summed >= 0, summed, 0.1 * summed).astype(BF).reshape(groups, inner, channels)
    now = act[:, 1 : 1 + piece].reshape(F_DEV, channels)
    keep_prev = (mine[:, :piece] == mine[:, 1 : 1 + piece])[:, :, None]
    keep_next = (mine[:, 2:] == mine[:, 1 : 1 + piece])[:, :, None]
    prev = jnp.where(keep_prev, act[:, :piece], jnp.zeros((), BF)).reshape(F_DEV, channels)
    nxt = jnp.where(keep_next, act[:, 2:], jnp.zeros((), BF)).reshape(F_DEV, channels)

    out_width = up_weight.shape[2]
    upsampled = upsample(now, prev, nxt, own_taps, other_taps)
    return upsampled.reshape(1, 1, groups, -1, out_width)


def upsample_kernel(now, prev, nxt, own, other, out, total):
    f32 = jnp.float32
    core = lax.rem(lax.axis_index("utt"), 2)

    def run(early, late):
        for r in range(8):
            if r < 4:
                value = jnp.dot(now[...], early[r + 4], preferred_element_type=f32)
                value += jnp.dot(prev[...], late[r + 4], preferred_element_type=f32)
            else:
                value = jnp.dot(now[...], late[r - 4], preferred_element_type=f32)
                value += jnp.dot(nxt[...], early[r - 4], preferred_element_type=f32)
            total[:, r, :] = value

    @pl.when(core == 0)
    def _():
        run(own, other)

    @pl.when(core == 1)
    def _():
        run(other, own)

    out[...] = total[...].astype(out.dtype)


def upsample(now, prev, nxt, early, late):
    frames, channels = now.shape
    width = early.shape[2]
    rows = 64
    tile = pl.BlockSpec((rows, channels), lambda i: (i, 0))
    whole = pl.BlockSpec((8, channels, width), lambda i: (0, 0, 0))
    return pl.pallas_call(
        upsample_kernel,
        grid=(frames // rows,),
        out_shape=jax.ShapeDtypeStruct((frames, 8, width), BF),
        in_specs=[tile, tile, tile, whole, whole],
        out_specs=pl.BlockSpec((rows, 8, width), lambda i: (i, 0, 0)),
        scratch_shapes=[pltpu.VMEM((rows, 8, width), jnp.float32)],
        name="upsample",
    )(now, prev, nxt, early, late)


def solution(mesh):
    placed = (
        P("utt", "tm"),
        P("utt", None),
        P("utt", None),
        P("utt", None),
        P("utt", "tm", None),
        P(),
        P(None, "tm"),
        P(None, "tm"),
        P(),
        P(),
        P(),
        P("tm", None, None),
    )
    return jax.shard_map(
        shards,
        mesh=mesh,
        in_specs=placed,
        out_specs=P("utt", "tm", None, None, None),
        check_vma=False,
    )
```

```python
import functools

import jax
import jax.numpy as jnp
from jax import lax
from jax.experimental import pallas as pl
from jax.experimental.pallas import tpu as pltpu
from jax.sharding import PartitionSpec as P

F_DEV = 256
SIDE = 8
WIDE = 128
REACH = 4
EPS = 1e-05
MESH = pl.DeviceIdType.MESH
BF = jnp.bfloat16


ORDER = (0, 1, 7, 2, 6, 3, 5, 4)


def gather_kernel(count, share, *refs):
    blocks = refs[:count]
    outs = refs[count : 2 * count]
    local_sem, first_send, first_recv, ring_send, ring_recv, pair_send, pair_recv = refs[2 * count :]
    utt = lax.axis_index("utt")
    tm = lax.axis_index("tm")
    core = lax.rem(utt, 2)
    pair = utt + 1 - 2 * core
    y = lax.div(tm, SIDE)
    z = lax.rem(tm, SIDE)
    first = y + core * (z - y)
    second = z + core * (y - z)
    half = core if share else 0

    def place(a, b):
        return a * SIDE + b + core * ((b - a) * SIDE + (a - b))

    def beside(step):
        return lax.rem(second + step + SIDE, SIDE)

    barrier = pltpu.get_barrier_semaphore()

    def greet(step, carry):
        pl.semaphore_signal(
            barrier, inc=1,
            device_id=(utt, place(lax.rem(first + step, SIDE), second)), device_id_type=MESH,
        )
        return carry

    lax.fori_loop(1, SIDE, greet, 0)
    for side in (1, -1):
        pl.semaphore_signal(
            barrier, inc=1, device_id=(utt, place(first, beside(side))), device_id_type=MESH
        )
    if share:
        pl.semaphore_signal(barrier, inc=1, device_id=(pair, tm), device_id_type=MESH)
    pl.semaphore_wait(barrier, SIDE + 1 + (1 if share else 0))

    own = [
        pltpu.make_async_copy(blocks[i], outs[i].at[half, second, first], local_sem.at[i])
        for i in range(count)
    ]

    def first_copy(i, step):
        return pltpu.make_async_remote_copy(
            src_ref=blocks[i],
            dst_ref=outs[i].at[half, second, first],
            send_sem=first_send.at[i, step],
            recv_sem=first_recv.at[i, step],
            device_id=(utt, place(lax.rem(first + step, SIDE), second)),
            device_id_type=MESH,
        )

    def ring_copy(i, way, step, order):
        side = 1 - 2 * way
        block = lax.rem(first - order + SIDE, SIDE)
        spot = outs[i].at[half, beside(-side * step), block]
        return pltpu.make_async_remote_copy(
            src_ref=spot,
            dst_ref=spot,
            send_sem=ring_send.at[i, way, step, order],
            recv_sem=ring_recv.at[i, way, step, order],
            device_id=(utt, place(first, beside(side))),
            device_id_type=MESH,
        )

    def pair_copy(i, step):
        row = outs[i].at[half, beside(step)]
        return pltpu.make_async_remote_copy(
            src_ref=row,
            dst_ref=row,
            send_sem=pair_send.at[i, step + 3],
            recv_sem=pair_recv.at[i, step + 3],
            device_id=(pair, tm),
            device_id_type=MESH,
        )

    def steps_of(way, order):
        return SIDE // 2 - (order + way) % 2

    for copy in own:
        copy.start()
    for step in ORDER[1:]:
        for i in range(count):
            first_copy(i, step).start()
    for copy in own:
        copy.wait()
    for order in ORDER:
        for i in range(count):
            if order > 0:
                first_copy(i, order).wait_recv()
            for way in range(2):
                ring_copy(i, way, 0, order).start()
    if share:
        for i in range(count):
            pair_copy(i, 0).start()
    for step in range(SIDE // 2):
        for order in ORDER:
            for i in range(count):
                for way in range(2):
                    if step < steps_of(way, order):
                        ring_copy(i, way, step, order).wait_recv()
                        if step + 1 < steps_of(way, order):
                            ring_copy(i, way, step + 1, order).start()
        if share:
            for i in range(count):
                pair_copy(i, -step - 1 if step < 3 else 4).start()
                if step < 3:
                    pair_copy(i, step + 1).start()
    for i in range(count):
        for order in ORDER:
            if order > 0:
                first_copy(i, order).wait_send()
            for way in range(2):
                for step in range(steps_of(way, order)):
                    ring_copy(i, way, step, order).wait_send()
    if share:
        for i in range(count):
            for step in range(-3, 5):
                pair_copy(i, step).wait()


def gather_blocks(blocks, share, number):
    count = len(blocks)
    halves = 2 if share else 1
    ring = (count, 2, SIDE // 2, SIDE)
    return pl.pallas_call(
        functools.partial(gather_kernel, count, share),
        out_shape=[
            jax.ShapeDtypeStruct((halves, SIDE, SIDE) + block.shape, block.dtype) for block in blocks
        ],
        in_specs=[pl.BlockSpec(memory_space=pl.ANY)] * count,
        out_specs=[pl.BlockSpec(memory_space=pl.ANY)] * count,
        scratch_shapes=[
            pltpu.SemaphoreType.DMA((count,)),
            pltpu.SemaphoreType.DMA((count, SIDE)),
            pltpu.SemaphoreType.DMA((count, SIDE)),
            pltpu.SemaphoreType.DMA(ring),
            pltpu.SemaphoreType.DMA(ring),
            pltpu.SemaphoreType.DMA((count, SIDE)),
            pltpu.SemaphoreType.DMA((count, SIDE)),
        ],
        compiler_params=pltpu.CompilerParams(collective_id=number, has_side_effects=True),
        name=f"gather{number}",
    )(*blocks)


def utterance_of(indices, bounds):
    return jnp.sum((bounds[None, :] <= indices[:, None]).astype(jnp.int32), axis=1)


def frame_layout(lasting, lengths, ordering):
    phone_total = lasting.shape[0]
    utt_count = lengths.shape[0]
    phone_index = jnp.arange(phone_total, dtype=jnp.int32)
    bounds = jnp.cumsum(lengths)
    utt_first = bounds - lengths
    inclusive = jnp.cumsum(lasting)
    exclusive = inclusive - lasting
    first_frame = jnp.take(exclusive, utt_first)
    utt_frames = jnp.take(inclusive, bounds - 1) - first_frame
    slots = jnp.arange(utt_count, dtype=jnp.int32)
    places = jnp.sum(jnp.where(ordering[None, :] == slots[:, None], slots[None, :], 0), axis=1)
    offsets = jnp.sum(jnp.where(places[None, :] < places[:, None], utt_frames[None, :], 0), axis=1)
    moved = offsets - first_frame
    member = (bounds[None, :] > phone_index[:, None]) & (utt_first[None, :] <= phone_index[:, None])
    starting = exclusive + jnp.sum(jnp.where(member, moved[None, :], 0), axis=1)
    return (starting, bounds)


def shards(
    phone_ids,
    durations,
    utt_lengths,
    utt_order,
    buckets,
    embed_table,
    conv1_weight,
    conv2_weight,
    norm_gain,
    mel_weight,
    pre_weight,
    up_weight,
):
    phone_count = phone_ids.shape[1]
    width = embed_table.shape[1]
    device = lax.axis_index("tm")
    core = lax.rem(lax.axis_index("utt"), 2)
    ends = lax.axis_size("tm") - 1

    symbols = embed_table.shape[0]
    filters_here = conv1_weight.shape[1]
    part = filters_here // 2
    pick = lambda both: jnp.where(core == 0, both[0], both[1])
    rising = pick(jnp.transpose(up_weight.reshape(up_weight.shape[0], 2, -1), (1, 0, 2)))
    inward = pick(conv1_weight.T.reshape(2, part, -1)).reshape(part * 9, width)
    inward = lax.dot_general(
        inward, embed_table, (((1,), (1,)), ((), ())), preferred_element_type=jnp.float32
    ).astype(BF)
    inward = jnp.pad(inward.reshape(part, 9 * symbols), ((0, 8 - part), (0, 0)))
    outward = jnp.pad(pick(conv2_weight.T.reshape(2, part, -1)), ((0, 8 - part), (0, 0)))
    both = jnp.concatenate([inward, outward], axis=1)
    both, rising = gather_blocks([both, rising], True, 1)
    both = both.reshape(2 * SIDE * SIDE * 8, -1)
    inward = both[:, : 9 * symbols]
    outward = both[:, 9 * symbols :]

    starting, bounds = frame_layout(durations[0], utt_lengths[0], utt_order[0])
    ending = starting + durations[0]
    nearby = device * phone_count + jnp.arange(-4, phone_count + 4, dtype=jnp.int32)
    phone_labels = jnp.where(nearby < 0, -1, utterance_of(nearby, bounds))
    head = lax.ppermute(phone_ids[0, :4], "tm", [(i + 1, i) for i in range(ends)])
    tail = lax.ppermute(phone_ids[0, -4:], "tm", [(i, i + 1) for i in range(ends)])
    ids = jnp.concatenate([tail, phone_ids[0], head])
    table = jnp.arange(symbols, dtype=jnp.int32)[None, :]
    chosen = (phone_ids[0][:, None] == table).astype(BF)
    embedded = jnp.dot(chosen, embed_table, preferred_element_type=jnp.float32)
    center = phone_labels[4 : 4 + phone_count]
    columns = []
    for tap in range(9):
        keep = phone_labels[tap : tap + phone_count] == center
        columns.append((jnp.where(keep, ids[tap : tap + phone_count], -1)[:, None] == table).astype(BF))
    unfolded = jnp.concatenate(columns, axis=1)
    filters = jnp.maximum(
        lax.dot_general(
            unfolded, inward, (((1,), (1,)), ((), ())), preferred_element_type=jnp.float32
        ),
        0.0,
    ).astype(BF)
    conv_out = jnp.dot(filters, outward, preferred_element_type=jnp.float32)
    resid = embedded + conv_out
    middle = jnp.mean(resid, axis=1, keepdims=True)
    spread = jnp.mean((resid - middle) ** 2, axis=1, keepdims=True)
    decoded = ((resid - middle) * lax.rsqrt(spread + EPS) * norm_gain[None, :]).astype(BF)
    mel_width = mel_weight.shape[1]
    mel_ph = jnp.dot(decoded, mel_weight, preferred_element_type=jnp.float32).astype(BF)
    lane = lax.broadcasted_iota(jnp.int32, (phone_count, WIDE), 1)
    told = jnp.where(lane == mel_width, (center + 1).astype(BF)[:, None], jnp.zeros((), BF))
    mel_block = jnp.pad(mel_ph, ((0, 0), (0, WIDE - mel_width))) + told
    (portion,) = gather_blocks([mel_block], False, 2)
    portion = portion.reshape(-1, WIDE)

    def arranged(values):
        cells = values.reshape(SIDE, SIDE, phone_count)
        return jnp.where(core == 0, jnp.transpose(cells, (1, 0, 2)), cells).reshape(-1)

    groups = lax.axis_size("utt")
    piece = F_DEV // groups
    span = piece + 2 * REACH
    slots = jnp.arange(groups, dtype=jnp.int32)
    source = jnp.sum(
        jnp.where(buckets[0, 0][None, :] == slots[:, None], slots[None, :], 0), axis=1
    )
    frames = (
        device * F_DEV + source[:, None] * piece - REACH
        + jnp.arange(span, dtype=jnp.int32)[None, :]
    ).reshape(-1)
    hit = (frames[:, None] >= arranged(starting)[None, :]) & (
        frames[:, None] < arranged(ending)[None, :]
    )
    windows = jnp.dot(hit.astype(BF), portion, preferred_element_type=jnp.float32).astype(BF)
    arrived = lax.all_to_all(
        windows.reshape(groups, span, WIDE), "utt", split_axis=0, concat_axis=0, tiled=True
    )

    labels = arrived[:, :, mel_width]
    channels = pre_weight.shape[2]
    pre_flat = jnp.pad(pre_weight, ((0, 0), (0, WIDE - mel_width), (0, 0))).reshape(-1, channels)
    inner = piece + 2
    mine = labels[:, 3 : 3 + inner]
    columns = []
    for tap in range(7):
        keep = (labels[:, tap : tap + inner] == mine)[:, :, None]
        columns.append(jnp.where(keep, arrived[:, tap : tap + inner], jnp.zeros((), BF)))
    unfolded = jnp.concatenate(columns, axis=2).reshape(groups * inner, -1)
    summed = jnp.dot(unfolded, pre_flat, preferred_element_type=jnp.float32)
    act = jnp.where(summed >= 0, summed, 0.1 * summed).astype(BF).reshape(groups, inner, channels)
    place = jnp.arange(channels, dtype=jnp.int32)
    unit = place // (SIDE * 8) * 8 + place // 8 % SIDE * (SIDE * 8) + place % 8
    turn = (place[:, None] == unit[None, :]).astype(BF)
    turned = jnp.dot(
        act.reshape(groups * inner, channels), turn, preferred_element_type=jnp.float32
    ).astype(BF).reshape(groups, inner, channels)
    keep_prev = (mine[:, :piece] == mine[:, 1 : 1 + piece])[:, :, None]
    keep_next = (mine[:, 2:] == mine[:, 1 : 1 + piece])[:, :, None]

    def windowed(cells, offset, keep=None):
        cells = cells[:, offset : offset + piece]
        if keep is not None:
            cells = jnp.where(keep, cells, jnp.zeros((), BF))
        return cells.reshape(F_DEV, channels)

    out_width = up_weight.shape[2]
    upsampled = upsample(
        windowed(turned, 1),
        windowed(act, 1),
        windowed(act, 0, keep_prev),
        windowed(turned, 2, keep_next),
        rising.reshape(2, channels, -1),
        out_width,
    )
    return upsampled.reshape(1, 1, groups, -1, out_width)


def upsample_kernel(early_now, late_now, prev, nxt, taps, out, total):
    f32 = jnp.float32
    width = out.shape[2]

    def tap(number):
        return taps[number // 8, :, pl.ds(number % 8 * width, width)]

    for r in range(8):
        if r < 4:
            value = jnp.dot(early_now[...], tap(r + 4), preferred_element_type=f32)
            value += jnp.dot(prev[...], tap(r + 12), preferred_element_type=f32)
        else:
            value = jnp.dot(late_now[...], tap(r + 4), preferred_element_type=f32)
            value += jnp.dot(nxt[...], tap(r - 4), preferred_element_type=f32)
        total[:, r, :] = value
    out[...] = total[...].astype(out.dtype)


def upsample(early_now, late_now, prev, nxt, taps, width):
    frames, channels = prev.shape
    rows = 64
    tile = pl.BlockSpec((rows, channels), lambda i: (i, 0))
    return pl.pallas_call(
        upsample_kernel,
        grid=(frames // rows,),
        out_shape=jax.ShapeDtypeStruct((frames, 8, width), BF),
        in_specs=[tile, tile, tile, tile, pl.BlockSpec(taps.shape, lambda i: (0, 0, 0))],
        out_specs=pl.BlockSpec((rows, 8, width), lambda i: (i, 0, 0)),
        scratch_shapes=[pltpu.VMEM((rows, 8, width), jnp.float32)],
        name="upsample",
    )(early_now, late_now, prev, nxt, taps)


def solution(mesh):
    placed = (
        P("utt", "tm"),
        P("utt", None),
        P("utt", None),
        P("utt", None),
        P("utt", "tm", None),
        P(),
        P(None, "tm"),
        P(None, "tm"),
        P(),
        P(),
        P(),
        P("tm", None, None),
    )
    return jax.shard_map(
        shards,
        mesh=mesh,
        in_specs=placed,
        out_specs=P("utt", "tm", None, None, None),
        check_vma=False,
    )
```

```python
import functools

import jax
import jax.numpy as jnp
from jax import lax
from jax.experimental import pallas as pl
from jax.experimental.pallas import tpu as pltpu
from jax.sharding import PartitionSpec as P

F_DEV = 256
SIDE = 8
WIDE = 128
REACH = 4
EPS = 1e-05
MESH = pl.DeviceIdType.MESH
BF = jnp.bfloat16


ORDER = (0, 1, 7, 2, 6, 3, 5, 4)


def gather_kernel(count, share, near, *refs):
    blocks = refs[:count]
    outs = refs[count + near : 2 * count + near]
    scratch = refs[2 * (count + near) :]
    local_sem, first_send, first_recv, ring_send, ring_recv, pair_send, pair_recv = scratch[:7]
    total = SIDE * SIDE
    utt = lax.axis_index("utt")
    tm = lax.axis_index("tm")
    core = lax.rem(utt, 2)
    pair = utt + 1 - 2 * core
    y = lax.div(tm, SIDE)
    z = lax.rem(tm, SIDE)
    first = y + core * (z - y)
    second = z + core * (y - z)
    half = core if share else 0

    def place(a, b):
        return a * SIDE + b + core * ((b - a) * SIDE + (a - b))

    def beside(step):
        return lax.rem(second + step + SIDE, SIDE)

    barrier = pltpu.get_barrier_semaphore()

    def greet(step, carry):
        pl.semaphore_signal(
            barrier, inc=1,
            device_id=(utt, place(lax.rem(first + step, SIDE), second)), device_id_type=MESH,
        )
        return carry

    lax.fori_loop(1, SIDE, greet, 0)
    for side in (1, -1):
        pl.semaphore_signal(
            barrier, inc=1, device_id=(utt, place(first, beside(side))), device_id_type=MESH
        )
    if share:
        pl.semaphore_signal(barrier, inc=1, device_id=(pair, tm), device_id_type=MESH)
    if near:
        for side in (1, total - 1):
            pl.semaphore_signal(
                barrier, inc=1, device_id=(utt, lax.rem(tm + side, total)), device_id_type=MESH
            )
    pl.semaphore_wait(barrier, SIDE + 1 + (1 if share else 0) + 2 * near)

    beside_copies = []
    if near:
        for spot, side in ((0, 1), (1, total - 1)):
            copy = pltpu.make_async_remote_copy(
                src_ref=refs[count],
                dst_ref=refs[2 * count + 1].at[spot],
                send_sem=scratch[7].at[spot],
                recv_sem=scratch[8].at[spot],
                device_id=(utt, lax.rem(tm + side, total)),
                device_id_type=MESH,
            )
            copy.start()
            beside_copies.append(copy)
    own = [
        pltpu.make_async_copy(blocks[i], outs[i].at[half, second, first], local_sem.at[i])
        for i in range(count)
    ]

    def first_copy(i, step):
        return pltpu.make_async_remote_copy(
            src_ref=blocks[i],
            dst_ref=outs[i].at[half, second, first],
            send_sem=first_send.at[i, step],
            recv_sem=first_recv.at[i, step],
            device_id=(utt, place(lax.rem(first + step, SIDE), second)),
            device_id_type=MESH,
        )

    def ring_copy(i, way, step, order):
        side = 1 - 2 * way
        block = lax.rem(first - order + SIDE, SIDE)
        spot = outs[i].at[half, beside(-side * step), block]
        return pltpu.make_async_remote_copy(
            src_ref=blocks[i] if step == 0 and order == 0 else spot,
            dst_ref=spot,
            send_sem=ring_send.at[i, way, step, order],
            recv_sem=ring_recv.at[i, way, step, order],
            device_id=(utt, place(first, beside(side))),
            device_id_type=MESH,
        )

    def pair_copy(i, step):
        row = outs[i].at[half, beside(step)]
        return pltpu.make_async_remote_copy(
            src_ref=row,
            dst_ref=row,
            send_sem=pair_send.at[i, step + 3],
            recv_sem=pair_recv.at[i, step + 3],
            device_id=(pair, tm),
            device_id_type=MESH,
        )

    def steps_of(way, order):
        return SIDE // 2 - (order + way) % 2

    for copy in own:
        copy.start()
    for step in ORDER[1:]:
        for i in range(count):
            first_copy(i, step).start()
    for order in ORDER:
        for i in range(count):
            if order > 0:
                first_copy(i, order).wait_recv()
            for way in range(2):
                ring_copy(i, way, 0, order).start()
    for copy in own:
        copy.wait()
    if share:
        for i in range(count):
            pair_copy(i, 0).start()
    for step in range(SIDE // 2):
        for order in ORDER:
            for i in range(count):
                for way in range(2):
                    if step < steps_of(way, order):
                        ring_copy(i, way, step, order).wait_recv()
                        if step + 1 < steps_of(way, order):
                            ring_copy(i, way, step + 1, order).start()
        if share:
            for i in range(count):
                pair_copy(i, -step - 1 if step < 3 else 4).start()
                if step < 3:
                    pair_copy(i, step + 1).start()
    for i in range(count):
        for order in ORDER:
            if order > 0:
                first_copy(i, order).wait_send()
            for way in range(2):
                for step in range(steps_of(way, order)):
                    ring_copy(i, way, step, order).wait_send()
    if share:
        for i in range(count):
            for step in range(-3, 5):
                pair_copy(i, step).wait()
    for copy in beside_copies:
        copy.wait()


def gather_blocks(blocks, share, number, beside=None):
    count = len(blocks)
    near = 0 if beside is None else 1
    halves = 2 if share else 1
    ring = (count, 2, SIDE // 2, SIDE)
    shapes = [
        jax.ShapeDtypeStruct((halves, SIDE, SIDE) + block.shape, block.dtype) for block in blocks
    ]
    scratch = [
        pltpu.SemaphoreType.DMA((count,)),
        pltpu.SemaphoreType.DMA((count, SIDE)),
        pltpu.SemaphoreType.DMA((count, SIDE)),
        pltpu.SemaphoreType.DMA(ring),
        pltpu.SemaphoreType.DMA(ring),
        pltpu.SemaphoreType.DMA((count, SIDE)),
        pltpu.SemaphoreType.DMA((count, SIDE)),
    ]
    operands = list(blocks)
    if near:
        operands.append(beside)
        shapes.append(jax.ShapeDtypeStruct((2,) + beside.shape, beside.dtype))
        scratch += [pltpu.SemaphoreType.DMA((2,)), pltpu.SemaphoreType.DMA((2,))]
    return pl.pallas_call(
        functools.partial(gather_kernel, count, share, near),
        out_shape=shapes,
        in_specs=[pl.BlockSpec(memory_space=pl.ANY)] * (count + near),
        out_specs=[pl.BlockSpec(memory_space=pl.ANY)] * (count + near),
        scratch_shapes=scratch,
        compiler_params=pltpu.CompilerParams(collective_id=number, has_side_effects=True),
        name=f"gather{number}",
    )(*operands)


def exchange_kernel(given, taken, local_sem, send_sem, recv_sem):
    utt = lax.axis_index("utt")
    tm = lax.axis_index("tm")
    groups = given.shape[0]
    barrier = pltpu.get_barrier_semaphore()
    for step in range(1, groups):
        pl.semaphore_signal(
            barrier, inc=1, device_id=(lax.rem(utt + step, groups), tm), device_id_type=MESH
        )
    pl.semaphore_wait(barrier, groups - 1)
    own = pltpu.make_async_copy(given.at[utt], taken.at[utt], local_sem)
    copies = []
    for step in range(1, groups):
        other = lax.rem(utt + step, groups)
        copy = pltpu.make_async_remote_copy(
            src_ref=given.at[other],
            dst_ref=taken.at[utt],
            send_sem=send_sem.at[step],
            recv_sem=recv_sem.at[step],
            device_id=(other, tm),
            device_id_type=MESH,
        )
        copy.start()
        copies.append(copy)
    own.start()
    own.wait()
    for copy in copies:
        copy.wait()


def exchange(windows, number):
    groups = windows.shape[0]
    return pl.pallas_call(
        exchange_kernel,
        out_shape=jax.ShapeDtypeStruct(windows.shape, windows.dtype),
        in_specs=[pl.BlockSpec(memory_space=pltpu.VMEM)],
        out_specs=pl.BlockSpec(memory_space=pltpu.VMEM),
        scratch_shapes=[
            pltpu.SemaphoreType.DMA,
            pltpu.SemaphoreType.DMA((groups,)),
            pltpu.SemaphoreType.DMA((groups,)),
        ],
        compiler_params=pltpu.CompilerParams(collective_id=number, has_side_effects=True),
        name="exchange",
    )(windows)


def utterance_of(indices, bounds):
    return jnp.sum((bounds[None, :] <= indices[:, None]).astype(jnp.int32), axis=1)


def frame_layout(lasting, lengths, ordering):
    phone_total = lasting.shape[0]
    utt_count = lengths.shape[0]
    phone_index = jnp.arange(phone_total, dtype=jnp.int32)
    bounds = jnp.cumsum(lengths)
    utt_first = bounds - lengths
    inclusive = jnp.cumsum(lasting)
    exclusive = inclusive - lasting
    first_frame = jnp.take(exclusive, utt_first)
    utt_frames = jnp.take(inclusive, bounds - 1) - first_frame
    slots = jnp.arange(utt_count, dtype=jnp.int32)
    places = jnp.sum(jnp.where(ordering[None, :] == slots[:, None], slots[None, :], 0), axis=1)
    offsets = jnp.sum(jnp.where(places[None, :] < places[:, None], utt_frames[None, :], 0), axis=1)
    moved = offsets - first_frame
    member = (bounds[None, :] > phone_index[:, None]) & (utt_first[None, :] <= phone_index[:, None])
    starting = exclusive + jnp.sum(jnp.where(member, moved[None, :], 0), axis=1)
    return (starting, bounds)


def shards(
    phone_ids,
    durations,
    utt_lengths,
    utt_order,
    buckets,
    embed_table,
    conv1_weight,
    conv2_weight,
    norm_gain,
    mel_weight,
    pre_weight,
    up_weight,
):
    phone_count = phone_ids.shape[1]
    width = embed_table.shape[1]
    device = lax.axis_index("tm")
    core = lax.rem(lax.axis_index("utt"), 2)

    symbols = embed_table.shape[0]
    filters_here = conv1_weight.shape[1]
    part = filters_here // 2
    pick = lambda both: jnp.where(core == 0, both[0], both[1])
    rising = pick(jnp.transpose(up_weight.reshape(up_weight.shape[0], 2, -1), (1, 0, 2)))
    inward = pick(conv1_weight.T.reshape(2, part, -1)).reshape(part * 9, width)
    inward = lax.dot_general(
        inward, embed_table, (((1,), (1,)), ((), ())), preferred_element_type=jnp.float32
    ).astype(BF)
    inward = jnp.pad(inward.reshape(part, 9 * symbols), ((0, 8 - part), (0, 0)))
    outward = jnp.pad(pick(conv2_weight.T.reshape(2, part, -1)), ((0, 8 - part), (0, 0)))
    both = jnp.concatenate([inward, outward], axis=1)
    both, rising, aside = gather_blocks([both, rising], True, 1, phone_ids)
    both = both.reshape(2 * SIDE * SIDE * 8, -1)
    inward = both[:, : 9 * symbols]
    outward = both[:, 9 * symbols :]

    starting, bounds = frame_layout(durations[0], utt_lengths[0], utt_order[0])
    ending = starting + durations[0]
    nearby = device * phone_count + jnp.arange(-4, phone_count + 4, dtype=jnp.int32)
    phone_labels = jnp.where(nearby < 0, -1, utterance_of(nearby, bounds))
    ids = jnp.concatenate([aside[0, 0, -4:], phone_ids[0], aside[1, 0, :4]])
    table = jnp.arange(symbols, dtype=jnp.int32)[None, :]
    chosen = (phone_ids[0][:, None] == table).astype(BF)
    embedded = jnp.dot(chosen, embed_table, preferred_element_type=jnp.float32)
    center = phone_labels[4 : 4 + phone_count]
    columns = []
    for tap in range(9):
        keep = phone_labels[tap : tap + phone_count] == center
        columns.append((jnp.where(keep, ids[tap : tap + phone_count], -1)[:, None] == table).astype(BF))
    unfolded = jnp.concatenate(columns, axis=1)
    filters = jnp.maximum(
        lax.dot_general(
            unfolded, inward, (((1,), (1,)), ((), ())), preferred_element_type=jnp.float32
        ),
        0.0,
    ).astype(BF)
    conv_out = jnp.dot(filters, outward, preferred_element_type=jnp.float32)
    resid = embedded + conv_out
    middle = jnp.mean(resid, axis=1, keepdims=True)
    spread = jnp.mean((resid - middle) ** 2, axis=1, keepdims=True)
    decoded = ((resid - middle) * lax.rsqrt(spread + EPS) * norm_gain[None, :]).astype(BF)
    mel_width = mel_weight.shape[1]
    mel_ph = jnp.dot(decoded, mel_weight, preferred_element_type=jnp.float32).astype(BF)
    lane = lax.broadcasted_iota(jnp.int32, (phone_count, WIDE), 1)
    told = jnp.where(lane == mel_width, (center + 1).astype(BF)[:, None], jnp.zeros((), BF))
    mel_block = jnp.pad(mel_ph, ((0, 0), (0, WIDE - mel_width))) + told
    (portion,) = gather_blocks([mel_block], False, 2)
    portion = portion.reshape(-1, WIDE)

    def arranged(values):
        cells = values.reshape(SIDE, SIDE, phone_count)
        return jnp.where(core == 0, jnp.transpose(cells, (1, 0, 2)), cells).reshape(-1)

    groups = lax.axis_size("utt")
    piece = F_DEV // groups
    span = piece + 2 * REACH
    slots = jnp.arange(groups, dtype=jnp.int32)
    source = jnp.sum(
        jnp.where(buckets[0, 0][None, :] == slots[:, None], slots[None, :], 0), axis=1
    )
    frames = (
        device * F_DEV + source[:, None] * piece - REACH
        + jnp.arange(span, dtype=jnp.int32)[None, :]
    ).reshape(-1)
    hit = (frames[:, None] >= arranged(starting)[None, :]) & (
        frames[:, None] < arranged(ending)[None, :]
    )
    windows = jnp.dot(hit.astype(BF), portion, preferred_element_type=jnp.float32).astype(BF)
    arrived = exchange(windows.reshape(groups, span, WIDE), 3)

    labels = arrived[:, :, mel_width]
    channels = pre_weight.shape[2]
    pre_flat = jnp.pad(pre_weight, ((0, 0), (0, WIDE - mel_width), (0, 0))).reshape(-1, channels)
    inner = piece + 2
    mine = labels[:, 3 : 3 + inner]
    columns = []
    for tap in range(7):
        keep = (labels[:, tap : tap + inner] == mine)[:, :, None]
        columns.append(jnp.where(keep, arrived[:, tap : tap + inner], jnp.zeros((), BF)))
    unfolded = jnp.concatenate(columns, axis=2).reshape(groups * inner, -1)
    summed = jnp.dot(unfolded, pre_flat, preferred_element_type=jnp.float32)
    act = jnp.where(summed >= 0, summed, 0.1 * summed).astype(BF).reshape(groups, inner, channels)
    place = jnp.arange(channels, dtype=jnp.int32)
    unit = place // (SIDE * 8) * 8 + place // 8 % SIDE * (SIDE * 8) + place % 8
    turn = (place[:, None] == unit[None, :]).astype(BF)
    turned = jnp.dot(
        act.reshape(groups * inner, channels), turn, preferred_element_type=jnp.float32
    ).astype(BF).reshape(groups, inner, channels)
    keep_prev = (mine[:, :piece] == mine[:, 1 : 1 + piece])[:, :, None]
    keep_next = (mine[:, 2:] == mine[:, 1 : 1 + piece])[:, :, None]

    def windowed(cells, offset, keep=None):
        cells = cells[:, offset : offset + piece]
        if keep is not None:
            cells = jnp.where(keep, cells, jnp.zeros((), BF))
        return cells.reshape(F_DEV, channels)

    out_width = up_weight.shape[2]
    upsampled = upsample(
        windowed(turned, 1),
        windowed(act, 1),
        windowed(act, 0, keep_prev),
        windowed(turned, 2, keep_next),
        rising.reshape(2, channels, -1),
        out_width,
    )
    return upsampled.reshape(1, 1, groups, -1, out_width)


def upsample_kernel(early_now, late_now, prev, nxt, taps, out, total):
    f32 = jnp.float32
    width = out.shape[2]

    def tap(number):
        return taps[number // 8, :, pl.ds(number % 8 * width, width)]

    for r in range(8):
        if r < 4:
            value = jnp.dot(early_now[...], tap(r + 4), preferred_element_type=f32)
            value += jnp.dot(prev[...], tap(r + 12), preferred_element_type=f32)
        else:
            value = jnp.dot(late_now[...], tap(r + 4), preferred_element_type=f32)
            value += jnp.dot(nxt[...], tap(r - 4), preferred_element_type=f32)
        total[:, r, :] = value
    out[...] = total[...].astype(out.dtype)


def upsample(early_now, late_now, prev, nxt, taps, width):
    frames, channels = prev.shape
    rows = 64
    tile = pl.BlockSpec((rows, channels), lambda i: (i, 0))
    return pl.pallas_call(
        upsample_kernel,
        grid=(frames // rows,),
        out_shape=jax.ShapeDtypeStruct((frames, 8, width), BF),
        in_specs=[tile, tile, tile, tile, pl.BlockSpec(taps.shape, lambda i: (0, 0, 0))],
        out_specs=pl.BlockSpec((rows, 8, width), lambda i: (i, 0, 0)),
        scratch_shapes=[pltpu.VMEM((rows, 8, width), jnp.float32)],
        name="upsample",
    )(early_now, late_now, prev, nxt, taps)


def solution(mesh):
    placed = (
        P("utt", "tm"),
        P("utt", None),
        P("utt", None),
        P("utt", None),
        P("utt", "tm", None),
        P(),
        P(None, "tm"),
        P(None, "tm"),
        P(),
        P(),
        P(),
        P("tm", None, None),
    )
    return jax.shard_map(
        shards,
        mesh=mesh,
        in_specs=placed,
        out_specs=P("utt", "tm", None, None, None),
        check_vma=False,
    )
```

```python
import functools

import jax
import jax.numpy as jnp
from jax import lax
from jax.experimental import pallas as pl
from jax.experimental.pallas import tpu as pltpu
from jax.sharding import PartitionSpec as P

F_DEV = 256
SIDE = 8
WIDE = 128
REACH = 4
EPS = 1e-05
MESH = pl.DeviceIdType.MESH
BF = jnp.bfloat16


ORDER = (0, 1, 7, 2, 6, 3, 5, 4)


def gather_kernel(count, share, near, *refs):
    blocks = refs[:count]
    outs = refs[count + near : 2 * count + near]
    scratch = refs[2 * (count + near) :]
    local_sem, first_send, first_recv, ring_send, ring_recv, pair_send, pair_recv = scratch[:7]
    total = SIDE * SIDE
    utt = lax.axis_index("utt")
    tm = lax.axis_index("tm")
    core = lax.rem(utt, 2)
    pair = utt + 1 - 2 * core
    y = lax.div(tm, SIDE)
    z = lax.rem(tm, SIDE)
    first = y + core * (z - y)
    second = z + core * (y - z)
    half = core if share else 0

    def place(a, b):
        return a * SIDE + b + core * ((b - a) * SIDE + (a - b))

    def beside(step):
        return lax.rem(second + step + SIDE, SIDE)

    barrier = pltpu.get_barrier_semaphore()

    def greet(step, carry):
        pl.semaphore_signal(
            barrier, inc=1,
            device_id=(utt, place(lax.rem(first + step, SIDE), second)), device_id_type=MESH,
        )
        return carry

    lax.fori_loop(1, SIDE, greet, 0)
    for side in (1, -1):
        pl.semaphore_signal(
            barrier, inc=1, device_id=(utt, place(first, beside(side))), device_id_type=MESH
        )
    if share:
        pl.semaphore_signal(barrier, inc=1, device_id=(pair, tm), device_id_type=MESH)
    if near:
        for side in (1, total - 1):
            pl.semaphore_signal(
                barrier, inc=1, device_id=(utt, lax.rem(tm + side, total)), device_id_type=MESH
            )
    pl.semaphore_wait(barrier, SIDE + 1 + (1 if share else 0) + 2 * near)

    beside_copies = []
    if near:
        for spot, side in ((0, 1), (1, total - 1)):
            copy = pltpu.make_async_remote_copy(
                src_ref=refs[count],
                dst_ref=refs[2 * count + 1].at[spot],
                send_sem=scratch[7].at[spot],
                recv_sem=scratch[8].at[spot],
                device_id=(utt, lax.rem(tm + side, total)),
                device_id_type=MESH,
            )
            copy.start()
            beside_copies.append(copy)
    own = [
        pltpu.make_async_copy(blocks[i], outs[i].at[half, second, first], local_sem.at[i])
        for i in range(count)
    ]

    def first_copy(i, step):
        return pltpu.make_async_remote_copy(
            src_ref=blocks[i],
            dst_ref=outs[i].at[half, second, first],
            send_sem=first_send.at[i, step],
            recv_sem=first_recv.at[i, step],
            device_id=(utt, place(lax.rem(first + step, SIDE), second)),
            device_id_type=MESH,
        )

    def ring_copy(i, way, step, order):
        side = 1 - 2 * way
        block = lax.rem(first - order + SIDE, SIDE)
        spot = outs[i].at[half, beside(-side * step), block]
        return pltpu.make_async_remote_copy(
            src_ref=blocks[i] if step == 0 and order == 0 else spot,
            dst_ref=spot,
            send_sem=ring_send.at[i, way, step, order],
            recv_sem=ring_recv.at[i, way, step, order],
            device_id=(utt, place(first, beside(side))),
            device_id_type=MESH,
        )

    def pair_copy(i, step):
        row = outs[i].at[half, beside(step)]
        return pltpu.make_async_remote_copy(
            src_ref=row,
            dst_ref=row,
            send_sem=pair_send.at[i, step + 3],
            recv_sem=pair_recv.at[i, step + 3],
            device_id=(pair, tm),
            device_id_type=MESH,
        )

    def steps_of(way, order):
        return SIDE // 2 - (order + way) % 2

    for copy in own:
        copy.start()
    for step in ORDER[1:]:
        for i in range(count):
            first_copy(i, step).start()
    for order in ORDER:
        for i in range(count):
            if order > 0:
                first_copy(i, order).wait_recv()
            for way in range(2):
                ring_copy(i, way, 0, order).start()
    for copy in own:
        copy.wait()
    if share:
        for i in range(count):
            pair_copy(i, 0).start()
    for step in range(SIDE // 2):
        for order in ORDER:
            for i in range(count):
                for way in range(2):
                    if step < steps_of(way, order):
                        ring_copy(i, way, step, order).wait_recv()
                        if step + 1 < steps_of(way, order):
                            ring_copy(i, way, step + 1, order).start()
        if share:
            for i in range(count):
                pair_copy(i, -step - 1 if step < 3 else 4).start()
                if step < 3:
                    pair_copy(i, step + 1).start()
    for i in range(count):
        for order in ORDER:
            if order > 0:
                first_copy(i, order).wait_send()
            for way in range(2):
                for step in range(steps_of(way, order)):
                    ring_copy(i, way, step, order).wait_send()
    if share:
        for i in range(count):
            for step in range(-3, 5):
                pair_copy(i, step).wait()
    for copy in beside_copies:
        copy.wait()


def gather_blocks(blocks, share, number, beside=None):
    count = len(blocks)
    near = 0 if beside is None else 1
    halves = 2 if share else 1
    ring = (count, 2, SIDE // 2, SIDE)
    shapes = [
        jax.ShapeDtypeStruct((halves, SIDE, SIDE) + block.shape, block.dtype) for block in blocks
    ]
    scratch = [
        pltpu.SemaphoreType.DMA((count,)),
        pltpu.SemaphoreType.DMA((count, SIDE)),
        pltpu.SemaphoreType.DMA((count, SIDE)),
        pltpu.SemaphoreType.DMA(ring),
        pltpu.SemaphoreType.DMA(ring),
        pltpu.SemaphoreType.DMA((count, SIDE)),
        pltpu.SemaphoreType.DMA((count, SIDE)),
    ]
    operands = list(blocks)
    if near:
        operands.append(beside)
        shapes.append(jax.ShapeDtypeStruct((2,) + beside.shape, beside.dtype))
        scratch += [pltpu.SemaphoreType.DMA((2,)), pltpu.SemaphoreType.DMA((2,))]
    return pl.pallas_call(
        functools.partial(gather_kernel, count, share, near),
        out_shape=shapes,
        in_specs=[pl.BlockSpec(memory_space=pl.ANY)] * (count + near),
        out_specs=[pl.BlockSpec(memory_space=pl.ANY)] * (count + near),
        scratch_shapes=scratch,
        compiler_params=pltpu.CompilerParams(collective_id=number, has_side_effects=True),
        name=f"gather{number}",
    )(*operands)


def exchange_kernel(given, taken, local_sem, send_sem, recv_sem):
    utt = lax.axis_index("utt")
    tm = lax.axis_index("tm")
    groups = given.shape[0]
    barrier = pltpu.get_barrier_semaphore()
    for step in range(1, groups):
        pl.semaphore_signal(
            barrier, inc=1, device_id=(lax.rem(utt + step, groups), tm), device_id_type=MESH
        )
    pl.semaphore_wait(barrier, groups - 1)
    own = pltpu.make_async_copy(given.at[utt], taken.at[utt], local_sem)
    copies = []
    for step in range(1, groups):
        other = lax.rem(utt + step, groups)
        copy = pltpu.make_async_remote_copy(
            src_ref=given.at[other],
            dst_ref=taken.at[utt],
            send_sem=send_sem.at[step],
            recv_sem=recv_sem.at[step],
            device_id=(other, tm),
            device_id_type=MESH,
        )
        copy.start()
        copies.append(copy)
    own.start()
    own.wait()
    for copy in copies:
        copy.wait()


def exchange(windows, number):
    groups = windows.shape[0]
    return pl.pallas_call(
        exchange_kernel,
        out_shape=jax.ShapeDtypeStruct(windows.shape, windows.dtype),
        in_specs=[pl.BlockSpec(memory_space=pltpu.VMEM)],
        out_specs=pl.BlockSpec(memory_space=pltpu.VMEM),
        scratch_shapes=[
            pltpu.SemaphoreType.DMA,
            pltpu.SemaphoreType.DMA((groups,)),
            pltpu.SemaphoreType.DMA((groups,)),
        ],
        compiler_params=pltpu.CompilerParams(collective_id=number, has_side_effects=True),
        name="exchange",
    )(windows)


def utterance_of(indices, bounds):
    return jnp.sum((bounds[None, :] <= indices[:, None]).astype(jnp.int32), axis=1)


def frame_layout(lasting, lengths, ordering):
    phone_total = lasting.shape[0]
    utt_count = lengths.shape[0]
    phone_index = jnp.arange(phone_total, dtype=jnp.int32)
    bounds = jnp.cumsum(lengths)
    utt_first = bounds - lengths
    inclusive = jnp.cumsum(lasting)
    exclusive = inclusive - lasting
    first_frame = jnp.take(exclusive, utt_first)
    utt_frames = jnp.take(inclusive, bounds - 1) - first_frame
    slots = jnp.arange(utt_count, dtype=jnp.int32)
    places = jnp.sum(jnp.where(ordering[None, :] == slots[:, None], slots[None, :], 0), axis=1)
    offsets = jnp.sum(jnp.where(places[None, :] < places[:, None], utt_frames[None, :], 0), axis=1)
    moved = offsets - first_frame
    member = (bounds[None, :] > phone_index[:, None]) & (utt_first[None, :] <= phone_index[:, None])
    starting = exclusive + jnp.sum(jnp.where(member, moved[None, :], 0), axis=1)
    return (starting, bounds)


def shards(
    phone_ids,
    durations,
    utt_lengths,
    utt_order,
    buckets,
    embed_table,
    conv1_weight,
    conv2_weight,
    norm_gain,
    mel_weight,
    pre_weight,
    up_weight,
):
    phone_count = phone_ids.shape[1]
    width = embed_table.shape[1]
    device = lax.axis_index("tm")
    core = lax.rem(lax.axis_index("utt"), 2)

    symbols = embed_table.shape[0]
    filters_here = conv1_weight.shape[1]
    part = filters_here // 2
    pick = lambda both: jnp.where(core == 0, both[0], both[1])
    rising = pick(jnp.transpose(up_weight.reshape(up_weight.shape[0], 2, -1), (1, 0, 2)))
    inward = pick(conv1_weight.T.reshape(2, part, -1)).reshape(part * 9, width)
    inward = lax.dot_general(
        inward, embed_table, (((1,), (1,)), ((), ())), preferred_element_type=jnp.float32
    ).astype(BF)
    inward = jnp.pad(inward.reshape(part, 9 * symbols), ((0, 8 - part), (0, 0)))
    outward = jnp.pad(pick(conv2_weight.T.reshape(2, part, -1)), ((0, 8 - part), (0, 0)))
    both = jnp.concatenate([inward, outward], axis=1)
    both, rising, aside = gather_blocks([both, rising], True, 1, phone_ids)
    both = both.reshape(2 * SIDE * SIDE * 8, -1)
    inward = both[:, : 9 * symbols]
    outward = both[:, 9 * symbols :]

    starting, bounds = frame_layout(durations[0], utt_lengths[0], utt_order[0])
    ending = starting + durations[0]
    nearby = device * phone_count + jnp.arange(-4, phone_count + 4, dtype=jnp.int32)
    phone_labels = jnp.where(nearby < 0, -1, utterance_of(nearby, bounds))
    ids = jnp.concatenate([aside[0, 0, -4:], phone_ids[0], aside[1, 0, :4]])
    table = jnp.arange(symbols, dtype=jnp.int32)[None, :]
    chosen = (phone_ids[0][:, None] == table).astype(BF)
    embedded = jnp.dot(chosen, embed_table, preferred_element_type=jnp.float32)
    center = phone_labels[4 : 4 + phone_count]
    columns = []
    for tap in range(9):
        keep = phone_labels[tap : tap + phone_count] == center
        columns.append((jnp.where(keep, ids[tap : tap + phone_count], -1)[:, None] == table).astype(BF))
    unfolded = jnp.concatenate(columns, axis=1)
    filters = jnp.maximum(
        lax.dot_general(
            unfolded, inward, (((1,), (1,)), ((), ())), preferred_element_type=jnp.float32
        ),
        0.0,
    ).astype(BF)
    conv_out = jnp.dot(filters, outward, preferred_element_type=jnp.float32)
    resid = embedded + conv_out
    middle = jnp.mean(resid, axis=1, keepdims=True)
    spread = jnp.mean((resid - middle) ** 2, axis=1, keepdims=True)
    decoded = ((resid - middle) * lax.rsqrt(spread + EPS) * norm_gain[None, :]).astype(BF)
    mel_width = mel_weight.shape[1]
    mel_ph = jnp.dot(decoded, mel_weight, preferred_element_type=jnp.float32).astype(BF)
    lane = lax.broadcasted_iota(jnp.int32, (phone_count, WIDE), 1)
    told = jnp.where(lane == mel_width, (center + 1).astype(BF)[:, None], jnp.zeros((), BF))
    mel_block = jnp.pad(mel_ph, ((0, 0), (0, WIDE - mel_width))) + told
    (portion,) = gather_blocks([mel_block], False, 2)
    portion = portion.reshape(-1, WIDE)

    def arranged(values):
        cells = values.reshape(SIDE, SIDE, phone_count)
        return jnp.where(core == 0, jnp.transpose(cells, (1, 0, 2)), cells).reshape(-1)

    groups = lax.axis_size("utt")
    piece = F_DEV // groups
    span = piece + 2 * REACH
    slots = jnp.arange(groups, dtype=jnp.int32)
    source = jnp.sum(
        jnp.where(buckets[0, 0][None, :] == slots[:, None], slots[None, :], 0), axis=1
    )
    frames = (
        device * F_DEV + source[:, None] * piece - REACH
        + jnp.arange(span, dtype=jnp.int32)[None, :]
    ).reshape(-1)
    hit = (frames[:, None] >= arranged(starting)[None, :]) & (
        frames[:, None] < arranged(ending)[None, :]
    )
    windows = jnp.dot(hit.astype(BF), portion, preferred_element_type=jnp.float32).astype(BF)
    arrived = exchange(windows.reshape(groups, span, WIDE), 3)

    out_width = up_weight.shape[2]
    channels = pre_weight.shape[2]
    upsampled = vocoder(
        arrived.reshape(groups * span, WIDE), pre_weight, rising.reshape(2, channels, -1),
        groups, piece, out_width,
    )
    return upsampled.reshape(1, 1, groups, -1, out_width)


def vocoder_kernel(groups, piece, cells_ref, pre, taps_ref, out, taps, total, sem):
    f32 = jnp.float32
    fetch = pltpu.make_async_copy(taps_ref, taps, sem)
    fetch.start()
    cells = cells_ref[...].astype(f32)
    rows = cells.shape[0]
    mel_width, channels = pre.shape[1:]
    width = out.shape[2]

    def ahead(values, steps):
        return values if steps == 0 else pltpu.roll(values, (rows - steps) % rows, 0)

    label = cells[:, mel_width : mel_width + 1]
    summed = jnp.zeros((rows, channels), f32)
    for tap in range(7):
        moved = ahead(cells, tap - 3)
        keep = moved[:, mel_width : mel_width + 1] == label
        kept = jnp.where(keep, moved, 0.0).astype(BF)
        summed += jnp.dot(kept[:, :mel_width], pre[tap], preferred_element_type=f32)
    act = jnp.where(summed >= 0, summed, 0.1 * summed).astype(BF)
    row = lax.broadcasted_iota(jnp.int32, (channels, channels), 0)
    place = lax.broadcasted_iota(jnp.int32, (channels, channels), 1)
    unit = (place // 64) * 8 + ((place // 8) % 8) * 64 + place % 8
    turn = jnp.where(row == unit, 1.0, 0.0).astype(BF)
    turned = jnp.dot(act, turn, preferred_element_type=f32)
    act = act.astype(f32)

    def windowed(values, offset):
        values = ahead(values, REACH + offset)
        if offset != 0:
            same = ahead(cells, REACH + offset) == ahead(cells, REACH)
            keep = jnp.where(same, 1.0, 0.0)[:, mel_width : mel_width + 1]
            values = jnp.where(keep > 0.5, values, 0.0)
        values = values.reshape(groups, rows // groups, channels)[:, :piece]
        return values.reshape(groups * piece, channels).astype(BF)

    late_now = windowed(act, 0)
    early_now = windowed(turned, 0)
    prev = windowed(act, -1)
    nxt = windowed(turned, 1)
    fetch.wait()

    def part(number):
        return taps[number // 8, :, pl.ds(number % 8 * width, width)]

    for r in range(8):
        if r < 4:
            value = jnp.dot(early_now, part(r + 4), preferred_element_type=f32)
            value += jnp.dot(prev, part(r + 12), preferred_element_type=f32)
        else:
            value = jnp.dot(late_now, part(r + 4), preferred_element_type=f32)
            value += jnp.dot(nxt, part(r - 4), preferred_element_type=f32)
        total[:, r, :] = value
    out[...] = total[...].astype(out.dtype)


def vocoder(cells, pre_weight, taps, groups, piece, width):
    vmem = pl.BlockSpec(memory_space=pltpu.VMEM)
    frames = groups * piece
    return pl.pallas_call(
        functools.partial(vocoder_kernel, groups, piece),
        out_shape=jax.ShapeDtypeStruct((frames, 8, width), BF),
        in_specs=[vmem, vmem, pl.BlockSpec(memory_space=pl.ANY)],
        out_specs=vmem,
        scratch_shapes=[
            pltpu.VMEM(taps.shape, taps.dtype),
            pltpu.VMEM((frames, 8, width), jnp.float32),
            pltpu.SemaphoreType.DMA,
        ],
        name="vocoder",
    )(cells, pre_weight, taps)


def solution(mesh):
    placed = (
        P("utt", "tm"),
        P("utt", None),
        P("utt", None),
        P("utt", None),
        P("utt", "tm", None),
        P(),
        P(None, "tm"),
        P(None, "tm"),
        P(),
        P(),
        P(),
        P("tm", None, None),
    )
    return jax.shard_map(
        shards,
        mesh=mesh,
        in_specs=placed,
        out_specs=P("utt", "tm", None, None, None),
        check_vma=False,
    )
```

```python
import functools

import jax
import jax.numpy as jnp
from jax import lax
from jax.experimental import pallas as pl
from jax.experimental.pallas import tpu as pltpu
from jax.sharding import PartitionSpec as P

F_DEV = 256
SIDE = 8
WIDE = 128
REACH = 4
EPS = 1e-05
MESH = pl.DeviceIdType.MESH
BF = jnp.bfloat16


ORDER = (0, 1, 7, 2, 6, 3, 5, 4)


def gather_kernel(count, share, near, *refs):
    blocks = refs[:count]
    outs = refs[count + near : 2 * count + near]
    scratch = refs[2 * (count + near) :]
    local_sem, first_send, first_recv, ring_send, ring_recv, pair_send, pair_recv = scratch[:7]
    total = SIDE * SIDE
    utt = lax.axis_index("utt")
    tm = lax.axis_index("tm")
    core = lax.rem(utt, 2)
    pair = utt + 1 - 2 * core
    y = lax.div(tm, SIDE)
    z = lax.rem(tm, SIDE)
    first = y + core * (z - y)
    second = z + core * (y - z)
    half = core if share else 0

    def place(a, b):
        return a * SIDE + b + core * ((b - a) * SIDE + (a - b))

    def beside(step):
        return lax.rem(second + step + SIDE, SIDE)

    barrier = pltpu.get_barrier_semaphore()

    for side in (1, SIDE - 1):
        pl.semaphore_signal(
            barrier, inc=1,
            device_id=(utt, place(lax.rem(first + side, SIDE), second)), device_id_type=MESH,
        )
    for side in (1, -1):
        pl.semaphore_signal(
            barrier, inc=1, device_id=(utt, place(first, beside(side))), device_id_type=MESH
        )
    if share:
        pl.semaphore_signal(barrier, inc=1, device_id=(pair, tm), device_id_type=MESH)
    if near:
        for side in (1, total - 1):
            pl.semaphore_signal(
                barrier, inc=1, device_id=(utt, lax.rem(tm + side, total)), device_id_type=MESH
            )
    pl.semaphore_wait(barrier, 4 + (1 if share else 0) + 2 * near)

    beside_copies = []
    if near:
        for spot, side in ((0, 1), (1, total - 1)):
            copy = pltpu.make_async_remote_copy(
                src_ref=refs[count],
                dst_ref=refs[2 * count + 1].at[spot],
                send_sem=scratch[7].at[spot],
                recv_sem=scratch[8].at[spot],
                device_id=(utt, lax.rem(tm + side, total)),
                device_id_type=MESH,
            )
            copy.start()
            beside_copies.append(copy)
    own = [
        pltpu.make_async_copy(blocks[i], outs[i].at[half, second, first], local_sem.at[i])
        for i in range(count)
    ]

    def first_copy(i, order):
        side = 1 if order <= SIDE // 2 else SIDE - 1
        back = order - 1 if side == 1 else order + 1
        block = lax.rem(first - back + 2 * SIDE, SIDE)
        spot = outs[i].at[half, second, block]
        return pltpu.make_async_remote_copy(
            src_ref=blocks[i] if back % SIDE == 0 else spot,
            dst_ref=spot,
            send_sem=first_send.at[i, order],
            recv_sem=first_recv.at[i, order],
            device_id=(utt, place(lax.rem(first + side, SIDE), second)),
            device_id_type=MESH,
        )

    def ring_copy(i, way, step, order):
        side = 1 - 2 * way
        block = lax.rem(first - order + SIDE, SIDE)
        spot = outs[i].at[half, beside(-side * step), block]
        return pltpu.make_async_remote_copy(
            src_ref=blocks[i] if step == 0 and order == 0 else spot,
            dst_ref=spot,
            send_sem=ring_send.at[i, way, step, order],
            recv_sem=ring_recv.at[i, way, step, order],
            device_id=(utt, place(first, beside(side))),
            device_id_type=MESH,
        )

    def pair_copy(i, step):
        row = outs[i].at[half, beside(step)]
        return pltpu.make_async_remote_copy(
            src_ref=row,
            dst_ref=row,
            send_sem=pair_send.at[i, step + 3],
            recv_sem=pair_recv.at[i, step + 3],
            device_id=(pair, tm),
            device_id_type=MESH,
        )

    def steps_of(way, order):
        return SIDE // 2 - (order + way) % 2

    for copy in own:
        copy.start()
    for i in range(count):
        for order in (1, SIDE - 1):
            first_copy(i, order).start()
    for order in ORDER:
        for i in range(count):
            if order > 0:
                first_copy(i, order).wait_recv()
                if order < SIDE // 2:
                    first_copy(i, order + 1).start()
                elif order > SIDE // 2 + 1:
                    first_copy(i, order - 1).start()
            for way in range(2):
                ring_copy(i, way, 0, order).start()
    for copy in own:
        copy.wait()
    if share:
        for i in range(count):
            pair_copy(i, 0).start()
    for step in range(SIDE // 2):
        for order in ORDER:
            for i in range(count):
                for way in range(2):
                    if step < steps_of(way, order):
                        ring_copy(i, way, step, order).wait_recv()
                        if step + 1 < steps_of(way, order):
                            ring_copy(i, way, step + 1, order).start()
        if share:
            for i in range(count):
                pair_copy(i, -step - 1 if step < 3 else 4).start()
                if step < 3:
                    pair_copy(i, step + 1).start()
    for i in range(count):
        for order in ORDER:
            if order > 0:
                first_copy(i, order).wait_send()
            for way in range(2):
                for step in range(steps_of(way, order)):
                    ring_copy(i, way, step, order).wait_send()
    if share:
        for i in range(count):
            for step in range(-3, 5):
                pair_copy(i, step).wait()
    for copy in beside_copies:
        copy.wait()


def gather_blocks(blocks, share, number, beside=None):
    count = len(blocks)
    near = 0 if beside is None else 1
    halves = 2 if share else 1
    ring = (count, 2, SIDE // 2, SIDE)
    shapes = [
        jax.ShapeDtypeStruct((halves, SIDE, SIDE) + block.shape, block.dtype) for block in blocks
    ]
    scratch = [
        pltpu.SemaphoreType.DMA((count,)),
        pltpu.SemaphoreType.DMA((count, SIDE)),
        pltpu.SemaphoreType.DMA((count, SIDE)),
        pltpu.SemaphoreType.DMA(ring),
        pltpu.SemaphoreType.DMA(ring),
        pltpu.SemaphoreType.DMA((count, SIDE)),
        pltpu.SemaphoreType.DMA((count, SIDE)),
    ]
    operands = list(blocks)
    if near:
        operands.append(beside)
        shapes.append(jax.ShapeDtypeStruct((2,) + beside.shape, beside.dtype))
        scratch += [pltpu.SemaphoreType.DMA((2,)), pltpu.SemaphoreType.DMA((2,))]
    return pl.pallas_call(
        functools.partial(gather_kernel, count, share, near),
        out_shape=shapes,
        in_specs=[pl.BlockSpec(memory_space=pl.ANY)] * (count + near),
        out_specs=[pl.BlockSpec(memory_space=pl.ANY)] * (count + near),
        scratch_shapes=scratch,
        compiler_params=pltpu.CompilerParams(collective_id=number, has_side_effects=True),
        name=f"gather{number}",
    )(*operands)


def exchange_kernel(given, taken, local_sem, send_sem, recv_sem):
    utt = lax.axis_index("utt")
    tm = lax.axis_index("tm")
    groups = given.shape[0]
    barrier = pltpu.get_barrier_semaphore()
    for step in range(1, groups):
        pl.semaphore_signal(
            barrier, inc=1, device_id=(lax.rem(utt + step, groups), tm), device_id_type=MESH
        )
    pl.semaphore_wait(barrier, groups - 1)
    own = pltpu.make_async_copy(given.at[utt], taken.at[utt], local_sem)
    copies = []
    for step in range(1, groups):
        other = lax.rem(utt + step, groups)
        copy = pltpu.make_async_remote_copy(
            src_ref=given.at[other],
            dst_ref=taken.at[utt],
            send_sem=send_sem.at[step],
            recv_sem=recv_sem.at[step],
            device_id=(other, tm),
            device_id_type=MESH,
        )
        copy.start()
        copies.append(copy)
    own.start()
    own.wait()
    for copy in copies:
        copy.wait()


def exchange(windows, number):
    groups = windows.shape[0]
    return pl.pallas_call(
        exchange_kernel,
        out_shape=jax.ShapeDtypeStruct(windows.shape, windows.dtype),
        in_specs=[pl.BlockSpec(memory_space=pltpu.VMEM)],
        out_specs=pl.BlockSpec(memory_space=pltpu.VMEM),
        scratch_shapes=[
            pltpu.SemaphoreType.DMA,
            pltpu.SemaphoreType.DMA((groups,)),
            pltpu.SemaphoreType.DMA((groups,)),
        ],
        compiler_params=pltpu.CompilerParams(collective_id=number, has_side_effects=True),
        name="exchange",
    )(windows)


def utterance_of(indices, bounds):
    return jnp.sum((bounds[None, :] <= indices[:, None]).astype(jnp.int32), axis=1)


def frame_layout(lasting, lengths, ordering):
    phone_total = lasting.shape[0]
    utt_count = lengths.shape[0]
    phone_index = jnp.arange(phone_total, dtype=jnp.int32)
    bounds = jnp.cumsum(lengths)
    utt_first = bounds - lengths
    inclusive = jnp.cumsum(lasting)
    exclusive = inclusive - lasting
    last_frame = jnp.take(inclusive, bounds - 1)
    first_frame = jnp.pad(last_frame, (1, 0))[:utt_count]
    utt_frames = last_frame - first_frame
    slots = jnp.arange(utt_count, dtype=jnp.int32)
    places = jnp.sum(jnp.where(ordering[None, :] == slots[:, None], slots[None, :], 0), axis=1)
    offsets = jnp.sum(jnp.where(places[None, :] < places[:, None], utt_frames[None, :], 0), axis=1)
    moved = offsets - first_frame
    member = (bounds[None, :] > phone_index[:, None]) & (utt_first[None, :] <= phone_index[:, None])
    starting = exclusive + jnp.sum(jnp.where(member, moved[None, :], 0), axis=1)
    return (starting, bounds)


def shards(
    phone_ids,
    durations,
    utt_lengths,
    utt_order,
    buckets,
    embed_table,
    conv1_weight,
    conv2_weight,
    norm_gain,
    mel_weight,
    pre_weight,
    up_weight,
):
    phone_count = phone_ids.shape[1]
    width = embed_table.shape[1]
    device = lax.axis_index("tm")
    core = lax.rem(lax.axis_index("utt"), 2)

    symbols = embed_table.shape[0]
    filters_here = conv1_weight.shape[1]
    part = filters_here // 2
    pick = lambda both: jnp.where(core == 0, both[0], both[1])
    rising = pick(jnp.transpose(up_weight.reshape(up_weight.shape[0], 2, -1), (1, 0, 2)))
    inward = pick(conv1_weight.T.reshape(2, part, -1)).reshape(part * 9, width)
    inward = lax.dot_general(
        inward, embed_table, (((1,), (1,)), ((), ())), preferred_element_type=jnp.float32
    ).astype(BF)
    inward = jnp.pad(inward.reshape(part, 9 * symbols), ((0, 8 - part), (0, 0)))
    outward = jnp.pad(pick(conv2_weight.T.reshape(2, part, -1)), ((0, 8 - part), (0, 0)))
    both = jnp.concatenate([inward, outward], axis=1)
    both, rising, aside = gather_blocks([both, rising], True, 1, phone_ids)
    both = both.reshape(2 * SIDE * SIDE * 8, -1)
    inward = both[:, : 9 * symbols]
    outward = both[:, 9 * symbols :]

    starting, bounds = frame_layout(durations[0], utt_lengths[0], utt_order[0])
    ending = starting + durations[0]
    nearby = device * phone_count + jnp.arange(-4, phone_count + 4, dtype=jnp.int32)
    phone_labels = jnp.where(nearby < 0, -1, utterance_of(nearby, bounds))
    ids = jnp.concatenate([aside[0, 0, -4:], phone_ids[0], aside[1, 0, :4]])
    table = jnp.arange(symbols, dtype=jnp.int32)[None, :]
    chosen = (phone_ids[0][:, None] == table).astype(BF)
    embedded = jnp.dot(chosen, embed_table, preferred_element_type=jnp.float32)
    center = phone_labels[4 : 4 + phone_count]
    columns = []
    for tap in range(9):
        keep = phone_labels[tap : tap + phone_count] == center
        columns.append((jnp.where(keep, ids[tap : tap + phone_count], -1)[:, None] == table).astype(BF))
    unfolded = jnp.concatenate(columns, axis=1)
    filters = jnp.maximum(
        lax.dot_general(
            unfolded, inward, (((1,), (1,)), ((), ())), preferred_element_type=jnp.float32
        ),
        0.0,
    ).astype(BF)
    conv_out = jnp.dot(filters, outward, preferred_element_type=jnp.float32)
    resid = embedded + conv_out
    middle = jnp.mean(resid, axis=1, keepdims=True)
    spread = jnp.mean((resid - middle) ** 2, axis=1, keepdims=True)
    decoded = ((resid - middle) * lax.rsqrt(spread + EPS) * norm_gain[None, :]).astype(BF)
    mel_width = mel_weight.shape[1]
    mel_ph = jnp.dot(decoded, mel_weight, preferred_element_type=jnp.float32).astype(BF)
    lane = lax.broadcasted_iota(jnp.int32, (phone_count, WIDE), 1)
    told = jnp.where(lane == mel_width, (center + 1).astype(BF)[:, None], jnp.zeros((), BF))
    mel_block = jnp.pad(mel_ph, ((0, 0), (0, WIDE - mel_width))) + told
    (portion,) = gather_blocks([mel_block], False, 2)
    portion = portion.reshape(-1, WIDE)

    def arranged(values):
        cells = values.reshape(SIDE, SIDE, phone_count)
        return jnp.where(core == 0, jnp.transpose(cells, (1, 0, 2)), cells).reshape(-1)

    groups = lax.axis_size("utt")
    piece = F_DEV // groups
    span = piece + 2 * REACH
    slots = jnp.arange(groups, dtype=jnp.int32)
    source = jnp.sum(
        jnp.where(buckets[0, 0][None, :] == slots[:, None], slots[None, :], 0), axis=1
    )
    frames = (
        device * F_DEV + source[:, None] * piece - REACH
        + jnp.arange(span, dtype=jnp.int32)[None, :]
    ).reshape(-1)
    hit = (frames[:, None] >= arranged(starting)[None, :]) & (
        frames[:, None] < arranged(ending)[None, :]
    )
    windows = jnp.dot(hit.astype(BF), portion, preferred_element_type=jnp.float32).astype(BF)
    arrived = exchange(windows.reshape(groups, span, WIDE), 3)

    out_width = up_weight.shape[2]
    channels = pre_weight.shape[2]
    upsampled = vocoder(
        arrived.reshape(groups * span, WIDE), pre_weight, rising.reshape(2, channels, -1),
        groups, piece, out_width,
    )
    return upsampled.reshape(1, 1, groups, -1, out_width)


def vocoder_kernel(groups, piece, cells_ref, pre, taps_ref, out, taps, total, sem):
    f32 = jnp.float32
    fetch = pltpu.make_async_copy(taps_ref, taps, sem)
    fetch.start()
    cells = cells_ref[...].astype(f32)
    rows = cells.shape[0]
    mel_width, channels = pre.shape[1:]
    width = out.shape[2]

    def ahead(values, steps):
        return values if steps == 0 else pltpu.roll(values, (rows - steps) % rows, 0)

    label = cells[:, mel_width : mel_width + 1]
    summed = jnp.zeros((rows, channels), f32)
    for tap in range(7):
        moved = ahead(cells, tap - 3)
        keep = moved[:, mel_width : mel_width + 1] == label
        kept = jnp.where(keep, moved, 0.0).astype(BF)
        summed += jnp.dot(kept[:, :mel_width], pre[tap], preferred_element_type=f32)
    act = jnp.where(summed >= 0, summed, 0.1 * summed).astype(BF)
    row = lax.broadcasted_iota(jnp.int32, (channels, channels), 0)
    place = lax.broadcasted_iota(jnp.int32, (channels, channels), 1)
    unit = (place // 64) * 8 + ((place // 8) % 8) * 64 + place % 8
    turn = jnp.where(row == unit, 1.0, 0.0).astype(BF)
    turned = jnp.dot(act, turn, preferred_element_type=f32)
    act = act.astype(f32)

    def windowed(values, offset):
        values = ahead(values, REACH + offset)
        if offset != 0:
            same = ahead(cells, REACH + offset) == ahead(cells, REACH)
            keep = jnp.where(same, 1.0, 0.0)[:, mel_width : mel_width + 1]
            values = jnp.where(keep > 0.5, values, 0.0)
        values = values.reshape(groups, rows // groups, channels)[:, :piece]
        return values.reshape(groups * piece, channels).astype(BF)

    late_now = windowed(act, 0)
    early_now = windowed(turned, 0)
    prev = windowed(act, -1)
    nxt = windowed(turned, 1)
    fetch.wait()

    def part(number):
        return taps[number // 8, :, pl.ds(number % 8 * width, width)]

    for r in range(8):
        if r < 4:
            value = jnp.dot(early_now, part(r + 4), preferred_element_type=f32)
            value += jnp.dot(prev, part(r + 12), preferred_element_type=f32)
        else:
            value = jnp.dot(late_now, part(r + 4), preferred_element_type=f32)
            value += jnp.dot(nxt, part(r - 4), preferred_element_type=f32)
        total[:, r, :] = value
    out[...] = total[...].astype(out.dtype)


def vocoder(cells, pre_weight, taps, groups, piece, width):
    vmem = pl.BlockSpec(memory_space=pltpu.VMEM)
    frames = groups * piece
    return pl.pallas_call(
        functools.partial(vocoder_kernel, groups, piece),
        out_shape=jax.ShapeDtypeStruct((frames, 8, width), BF),
        in_specs=[vmem, vmem, pl.BlockSpec(memory_space=pl.ANY)],
        out_specs=vmem,
        scratch_shapes=[
            pltpu.VMEM(taps.shape, taps.dtype),
            pltpu.VMEM((frames, 8, width), jnp.float32),
            pltpu.SemaphoreType.DMA,
        ],
        name="vocoder",
    )(cells, pre_weight, taps)


def solution(mesh):
    placed = (
        P("utt", "tm"),
        P("utt", None),
        P("utt", None),
        P("utt", None),
        P("utt", "tm", None),
        P(),
        P(None, "tm"),
        P(None, "tm"),
        P(),
        P(),
        P(),
        P("tm", None, None),
    )
    return jax.shard_map(
        shards,
        mesh=mesh,
        in_specs=placed,
        out_specs=P("utt", "tm", None, None, None),
        check_vma=False,
    )
```

```python
import functools

import jax
import jax.numpy as jnp
from jax import lax
from jax.experimental import pallas as pl
from jax.experimental.pallas import tpu as pltpu
from jax.sharding import PartitionSpec as P

F_DEV = 256
SIDE = 8
WIDE = 128
REACH = 4
EPS = 1e-05
MESH = pl.DeviceIdType.MESH
BF = jnp.bfloat16


ORDER = (0, 1, 7, 2, 6, 3, 5, 4)


def gather_kernel(count, share, near, *refs):
    blocks = refs[:count]
    outs = refs[count + near : 2 * count + near]
    scratch = refs[2 * (count + near) :]
    local_sem, first_send, first_recv, ring_send, ring_recv, pair_send, pair_recv = scratch[:7]
    total = SIDE * SIDE
    utt = lax.axis_index("utt")
    tm = lax.axis_index("tm")
    core = lax.rem(utt, 2)
    pair = utt + 1 - 2 * core
    y = lax.div(tm, SIDE)
    z = lax.rem(tm, SIDE)
    first = y + core * (z - y)
    second = z + core * (y - z)
    half = core if share else 0

    def place(a, b):
        return a * SIDE + b + core * ((b - a) * SIDE + (a - b))

    def beside(step):
        return lax.rem(second + step + SIDE, SIDE)

    barrier = pltpu.get_barrier_semaphore()

    def greet(step, carry):
        pl.semaphore_signal(
            barrier, inc=1,
            device_id=(utt, place(lax.rem(first + step, SIDE), second)), device_id_type=MESH,
        )
        return carry

    lax.fori_loop(1, SIDE, greet, 0)
    for side in (1, -1):
        pl.semaphore_signal(
            barrier, inc=1, device_id=(utt, place(first, beside(side))), device_id_type=MESH
        )
    if share:
        pl.semaphore_signal(barrier, inc=1, device_id=(pair, tm), device_id_type=MESH)
    if near:
        for side in (1, total - 1):
            pl.semaphore_signal(
                barrier, inc=1, device_id=(utt, lax.rem(tm + side, total)), device_id_type=MESH
            )
    pl.semaphore_wait(barrier, SIDE + 1 + (1 if share else 0) + 2 * near)

    beside_copies = []
    if near:
        for spot, side in ((0, 1), (1, total - 1)):
            copy = pltpu.make_async_remote_copy(
                src_ref=refs[count],
                dst_ref=refs[2 * count + 1].at[spot],
                send_sem=scratch[7].at[spot],
                recv_sem=scratch[8].at[spot],
                device_id=(utt, lax.rem(tm + side, total)),
                device_id_type=MESH,
            )
            copy.start()
            beside_copies.append(copy)
    own = [
        pltpu.make_async_copy(blocks[i], outs[i].at[half, second, first], local_sem.at[i])
        for i in range(count)
    ]

    def first_copy(i, step):
        return pltpu.make_async_remote_copy(
            src_ref=blocks[i],
            dst_ref=outs[i].at[half, second, first],
            send_sem=first_send.at[i, step],
            recv_sem=first_recv.at[i, step],
            device_id=(utt, place(lax.rem(first + step, SIDE), second)),
            device_id_type=MESH,
        )

    def ring_copy(i, way, step, order):
        side = 1 - 2 * way
        block = lax.rem(first - order + SIDE, SIDE)
        spot = outs[i].at[half, beside(-side * step), block]
        return pltpu.make_async_remote_copy(
            src_ref=blocks[i] if step == 0 and order == 0 else spot,
            dst_ref=spot,
            send_sem=ring_send.at[i, way, step, order],
            recv_sem=ring_recv.at[i, way, step, order],
            device_id=(utt, place(first, beside(side))),
            device_id_type=MESH,
        )

    def pair_copy(i, step):
        row = outs[i].at[half, beside(step)]
        return pltpu.make_async_remote_copy(
            src_ref=row,
            dst_ref=row,
            send_sem=pair_send.at[i, step + 3],
            recv_sem=pair_recv.at[i, step + 3],
            device_id=(pair, tm),
            device_id_type=MESH,
        )

    def steps_of(way, order):
        return SIDE // 2 - (order + way) % 2

    for copy in own:
        copy.start()
    for step in ORDER[1:]:
        for i in range(count):
            first_copy(i, step).start()
    for order in ORDER:
        for i in range(count):
            if order > 0:
                first_copy(i, order).wait_recv()
            for way in range(2):
                ring_copy(i, way, 0, order).start()
    for copy in own:
        copy.wait()
    if share:
        for i in range(count):
            pair_copy(i, 0).start()
    for step in range(SIDE // 2):
        for order in ORDER:
            for i in range(count):
                for way in range(2):
                    if step < steps_of(way, order):
                        ring_copy(i, way, step, order).wait_recv()
                        if step + 1 < steps_of(way, order):
                            ring_copy(i, way, step + 1, order).start()
        if share:
            for i in range(count):
                pair_copy(i, -step - 1 if step < 3 else 4).start()
                if step < 3:
                    pair_copy(i, step + 1).start()
    for i in range(count):
        for order in ORDER:
            if order > 0:
                first_copy(i, order).wait_send()
            for way in range(2):
                for step in range(steps_of(way, order)):
                    ring_copy(i, way, step, order).wait_send()
    if share:
        for i in range(count):
            for step in range(-3, 5):
                pair_copy(i, step).wait()
    for copy in beside_copies:
        copy.wait()


def gather_blocks(blocks, share, number, space, beside=None):
    count = len(blocks)
    near = 0 if beside is None else 1
    halves = 2 if share else 1
    ring = (count, 2, SIDE // 2, SIDE)
    shapes = [
        jax.ShapeDtypeStruct((halves, SIDE, SIDE) + block.shape, block.dtype) for block in blocks
    ]
    scratch = [
        pltpu.SemaphoreType.DMA((count,)),
        pltpu.SemaphoreType.DMA((count, SIDE)),
        pltpu.SemaphoreType.DMA((count, SIDE)),
        pltpu.SemaphoreType.DMA(ring),
        pltpu.SemaphoreType.DMA(ring),
        pltpu.SemaphoreType.DMA((count, SIDE)),
        pltpu.SemaphoreType.DMA((count, SIDE)),
    ]
    operands = list(blocks)
    if near:
        operands.append(beside)
        shapes.append(jax.ShapeDtypeStruct((2,) + beside.shape, beside.dtype))
        scratch += [pltpu.SemaphoreType.DMA((2,)), pltpu.SemaphoreType.DMA((2,))]
    return pl.pallas_call(
        functools.partial(gather_kernel, count, share, near),
        out_shape=shapes,
        in_specs=[pl.BlockSpec(memory_space=space)] * (count + near),
        out_specs=[pl.BlockSpec(memory_space=space)] * (count + near),
        scratch_shapes=scratch,
        compiler_params=pltpu.CompilerParams(collective_id=number, has_side_effects=True),
        name=f"gather{number}",
    )(*operands)


def exchange_kernel(given, taken, local_sem, send_sem, recv_sem):
    utt = lax.axis_index("utt")
    tm = lax.axis_index("tm")
    groups = given.shape[0]
    barrier = pltpu.get_barrier_semaphore()
    for step in range(1, groups):
        pl.semaphore_signal(
            barrier, inc=1, device_id=(lax.rem(utt + step, groups), tm), device_id_type=MESH
        )
    pl.semaphore_wait(barrier, groups - 1)
    own = pltpu.make_async_copy(given.at[utt], taken.at[utt], local_sem)
    copies = []
    for step in range(1, groups):
        other = lax.rem(utt + step, groups)
        copy = pltpu.make_async_remote_copy(
            src_ref=given.at[other],
            dst_ref=taken.at[utt],
            send_sem=send_sem.at[step],
            recv_sem=recv_sem.at[step],
            device_id=(other, tm),
            device_id_type=MESH,
        )
        copy.start()
        copies.append(copy)
    own.start()
    own.wait()
    for copy in copies:
        copy.wait()


def exchange(windows, number):
    groups = windows.shape[0]
    return pl.pallas_call(
        exchange_kernel,
        out_shape=jax.ShapeDtypeStruct(windows.shape, windows.dtype),
        in_specs=[pl.BlockSpec(memory_space=pltpu.VMEM)],
        out_specs=pl.BlockSpec(memory_space=pltpu.VMEM),
        scratch_shapes=[
            pltpu.SemaphoreType.DMA,
            pltpu.SemaphoreType.DMA((groups,)),
            pltpu.SemaphoreType.DMA((groups,)),
        ],
        compiler_params=pltpu.CompilerParams(collective_id=number, has_side_effects=True),
        name="exchange",
    )(windows)


def utterance_of(indices, bounds):
    return jnp.sum((bounds[None, :] <= indices[:, None]).astype(jnp.int32), axis=1)


def frame_layout(lasting, lengths, ordering):
    phone_total = lasting.shape[0]
    utt_count = lengths.shape[0]
    phone_index = jnp.arange(phone_total, dtype=jnp.int32)
    bounds = jnp.cumsum(lengths)
    utt_first = bounds - lengths
    inclusive = jnp.cumsum(lasting)
    exclusive = inclusive - lasting
    last_frame = jnp.take(inclusive, bounds - 1)
    first_frame = jnp.pad(last_frame, (1, 0))[:utt_count]
    utt_frames = last_frame - first_frame
    slots = jnp.arange(utt_count, dtype=jnp.int32)
    places = jnp.sum(jnp.where(ordering[None, :] == slots[:, None], slots[None, :], 0), axis=1)
    offsets = jnp.sum(jnp.where(places[None, :] < places[:, None], utt_frames[None, :], 0), axis=1)
    moved = offsets - first_frame
    member = (bounds[None, :] > phone_index[:, None]) & (utt_first[None, :] <= phone_index[:, None])
    starting = exclusive + jnp.sum(jnp.where(member, moved[None, :], 0), axis=1)
    return (starting, bounds)


def shards(
    phone_ids,
    durations,
    utt_lengths,
    utt_order,
    buckets,
    embed_table,
    conv1_weight,
    conv2_weight,
    norm_gain,
    mel_weight,
    pre_weight,
    up_weight,
):
    phone_count = phone_ids.shape[1]
    width = embed_table.shape[1]
    device = lax.axis_index("tm")
    core = lax.rem(lax.axis_index("utt"), 2)

    symbols = embed_table.shape[0]
    filters_here = conv1_weight.shape[1]
    part = filters_here // 2
    pick = lambda both: jnp.where(core == 0, both[0], both[1])
    rising = pick(jnp.transpose(up_weight.reshape(up_weight.shape[0], 2, -1), (1, 0, 2)))
    inward = pick(conv1_weight.T.reshape(2, part, -1)).reshape(part * 9, width)
    inward = lax.dot_general(
        inward, embed_table, (((1,), (1,)), ((), ())), preferred_element_type=jnp.float32
    ).astype(BF)
    inward = jnp.pad(inward.reshape(part, 9 * symbols), ((0, 8 - part), (0, 0)))
    outward = jnp.pad(pick(conv2_weight.T.reshape(2, part, -1)), ((0, 8 - part), (0, 0)))
    both = jnp.concatenate([inward, outward], axis=1)
    both, rising, aside = gather_blocks([both, rising], True, 1, pl.ANY, phone_ids)
    both = both.reshape(2 * SIDE * SIDE * 8, -1)
    inward = both[:, : 9 * symbols]
    outward = both[:, 9 * symbols :]

    starting, bounds = frame_layout(durations[0], utt_lengths[0], utt_order[0])
    ending = starting + durations[0]
    nearby = device * phone_count + jnp.arange(-4, phone_count + 4, dtype=jnp.int32)
    phone_labels = jnp.where(nearby < 0, -1, utterance_of(nearby, bounds))
    ids = jnp.concatenate([aside[0, 0, -4:], phone_ids[0], aside[1, 0, :4]])
    table = jnp.arange(symbols, dtype=jnp.int32)[None, :]
    chosen = (phone_ids[0][:, None] == table).astype(BF)
    embedded = jnp.dot(chosen, embed_table, preferred_element_type=jnp.float32)
    center = phone_labels[4 : 4 + phone_count]
    columns = []
    for tap in range(9):
        keep = phone_labels[tap : tap + phone_count] == center
        columns.append((jnp.where(keep, ids[tap : tap + phone_count], -1)[:, None] == table).astype(BF))
    unfolded = jnp.concatenate(columns, axis=1)
    filters = jnp.maximum(
        lax.dot_general(
            unfolded, inward, (((1,), (1,)), ((), ())), preferred_element_type=jnp.float32
        ),
        0.0,
    ).astype(BF)
    conv_out = jnp.dot(filters, outward, preferred_element_type=jnp.float32)
    resid = embedded + conv_out
    middle = jnp.mean(resid, axis=1, keepdims=True)
    spread = jnp.mean((resid - middle) ** 2, axis=1, keepdims=True)
    decoded = ((resid - middle) * lax.rsqrt(spread + EPS) * norm_gain[None, :]).astype(BF)
    mel_width = mel_weight.shape[1]
    mel_ph = jnp.dot(decoded, mel_weight, preferred_element_type=jnp.float32).astype(BF)
    lane = lax.broadcasted_iota(jnp.int32, (phone_count, WIDE), 1)
    told = jnp.where(lane == mel_width, (center + 1).astype(BF)[:, None], jnp.zeros((), BF))
    mel_block = jnp.pad(mel_ph, ((0, 0), (0, WIDE - mel_width))) + told
    (portion,) = gather_blocks([mel_block], False, 2, pltpu.VMEM)
    portion = portion.reshape(-1, WIDE)

    def arranged(values):
        cells = values.reshape(SIDE, SIDE, phone_count)
        return jnp.where(core == 0, jnp.transpose(cells, (1, 0, 2)), cells).reshape(-1)

    groups = lax.axis_size("utt")
    piece = F_DEV // groups
    span = piece + 2 * REACH
    slots = jnp.arange(groups, dtype=jnp.int32)
    source = jnp.sum(
        jnp.where(buckets[0, 0][None, :] == slots[:, None], slots[None, :], 0), axis=1
    )
    frames = (
        device * F_DEV + source[:, None] * piece - REACH
        + jnp.arange(span, dtype=jnp.int32)[None, :]
    ).reshape(-1)
    hit = (frames[:, None] >= arranged(starting)[None, :]) & (
        frames[:, None] < arranged(ending)[None, :]
    )
    windows = jnp.dot(hit.astype(BF), portion, preferred_element_type=jnp.float32).astype(BF)
    arrived = exchange(windows.reshape(groups, span, WIDE), 3)

    out_width = up_weight.shape[2]
    channels = pre_weight.shape[2]
    upsampled = vocoder(
        arrived.reshape(groups * span, WIDE), pre_weight, rising.reshape(2, channels, -1),
        groups, piece, out_width,
    )
    return upsampled.reshape(1, 1, groups, -1, out_width)


def vocoder_kernel(groups, piece, cells_ref, pre, taps_ref, out, taps, total, sem):
    f32 = jnp.float32
    fetch = pltpu.make_async_copy(taps_ref, taps, sem)
    fetch.start()
    cells = cells_ref[...].astype(f32)
    rows = cells.shape[0]
    mel_width, channels = pre.shape[1:]
    width = out.shape[2]

    def ahead(values, steps):
        return values if steps == 0 else pltpu.roll(values, (rows - steps) % rows, 0)

    label = cells[:, mel_width : mel_width + 1]
    summed = jnp.zeros((rows, channels), f32)
    for tap in range(7):
        moved = ahead(cells, tap - 3)
        keep = moved[:, mel_width : mel_width + 1] == label
        kept = jnp.where(keep, moved, 0.0).astype(BF)
        summed += jnp.dot(kept[:, :mel_width], pre[tap], preferred_element_type=f32)
    act = jnp.where(summed >= 0, summed, 0.1 * summed).astype(BF)
    row = lax.broadcasted_iota(jnp.int32, (channels, channels), 0)
    place = lax.broadcasted_iota(jnp.int32, (channels, channels), 1)
    unit = (place // 64) * 8 + ((place // 8) % 8) * 64 + place % 8
    turn = jnp.where(row == unit, 1.0, 0.0).astype(BF)
    turned = jnp.dot(act, turn, preferred_element_type=f32)
    act = act.astype(f32)

    def windowed(values, offset):
        values = ahead(values, REACH + offset)
        if offset != 0:
            same = ahead(cells, REACH + offset) == ahead(cells, REACH)
            keep = jnp.where(same, 1.0, 0.0)[:, mel_width : mel_width + 1]
            values = jnp.where(keep > 0.5, values, 0.0)
        values = values.reshape(groups, rows // groups, channels)[:, :piece]
        return values.reshape(groups * piece, channels).astype(BF)

    late_now = windowed(act, 0)
    early_now = windowed(turned, 0)
    prev = windowed(act, -1)
    nxt = windowed(turned, 1)
    fetch.wait()

    def part(number):
        return taps[number // 8, :, pl.ds(number % 8 * width, width)]

    for r in range(8):
        if r < 4:
            value = jnp.dot(early_now, part(r + 4), preferred_element_type=f32)
            value += jnp.dot(prev, part(r + 12), preferred_element_type=f32)
        else:
            value = jnp.dot(late_now, part(r + 4), preferred_element_type=f32)
            value += jnp.dot(nxt, part(r - 4), preferred_element_type=f32)
        total[:, r, :] = value
    out[...] = total[...].astype(out.dtype)


def vocoder(cells, pre_weight, taps, groups, piece, width):
    vmem = pl.BlockSpec(memory_space=pltpu.VMEM)
    frames = groups * piece
    return pl.pallas_call(
        functools.partial(vocoder_kernel, groups, piece),
        out_shape=jax.ShapeDtypeStruct((frames, 8, width), BF),
        in_specs=[vmem, vmem, pl.BlockSpec(memory_space=pl.ANY)],
        out_specs=vmem,
        scratch_shapes=[
            pltpu.VMEM(taps.shape, taps.dtype),
            pltpu.VMEM((frames, 8, width), jnp.float32),
            pltpu.SemaphoreType.DMA,
        ],
        name="vocoder",
    )(cells, pre_weight, taps)


def solution(mesh):
    placed = (
        P("utt", "tm"),
        P("utt", None),
        P("utt", None),
        P("utt", None),
        P("utt", "tm", None),
        P(),
        P(None, "tm"),
        P(None, "tm"),
        P(),
        P(),
        P(),
        P("tm", None, None),
    )
    return jax.shard_map(
        shards,
        mesh=mesh,
        in_specs=placed,
        out_specs=P("utt", "tm", None, None, None),
        check_vma=False,
    )
```

```python
import functools

import jax
import jax.numpy as jnp
from jax import lax
from jax.experimental import pallas as pl
from jax.experimental.pallas import tpu as pltpu
from jax.sharding import PartitionSpec as P

F_DEV = 256
SIDE = 8
WIDE = 128
REACH = 4
EPS = 1e-05
MESH = pl.DeviceIdType.MESH
BF = jnp.bfloat16


ORDER = (0, 1, 7, 2, 6, 3, 5, 4)


def gather_kernel(count, share, near, *refs):
    blocks = refs[:count]
    outs = refs[count + near : 2 * count + near]
    scratch = refs[2 * (count + near) :]
    local_sem, first_send, first_recv, ring_send, ring_recv, pair_send, pair_recv = scratch[:7]
    total = SIDE * SIDE
    utt = lax.axis_index("utt")
    tm = lax.axis_index("tm")
    core = lax.rem(utt, 2)
    pair = utt + 1 - 2 * core
    y = lax.div(tm, SIDE)
    z = lax.rem(tm, SIDE)
    first = y + core * (z - y)
    second = z + core * (y - z)
    half = core if share else 0

    def place(a, b):
        return a * SIDE + b + core * ((b - a) * SIDE + (a - b))

    def beside(step):
        return lax.rem(second + step + SIDE, SIDE)

    barrier = pltpu.get_barrier_semaphore()

    def greet(step, carry):
        pl.semaphore_signal(
            barrier, inc=1,
            device_id=(utt, place(lax.rem(first + step, SIDE), second)), device_id_type=MESH,
        )
        return carry

    lax.fori_loop(1, SIDE, greet, 0)
    leap = not share
    for side in (1, -1, 2, -2) if leap else (1, -1):
        pl.semaphore_signal(
            barrier, inc=1, device_id=(utt, place(first, beside(side))), device_id_type=MESH
        )
    if share:
        pl.semaphore_signal(barrier, inc=1, device_id=(pair, tm), device_id_type=MESH)
    if near:
        for side in (1, total - 1):
            pl.semaphore_signal(
                barrier, inc=1, device_id=(utt, lax.rem(tm + side, total)), device_id_type=MESH
            )
    pl.semaphore_wait(barrier, SIDE + (1 if share else 3) + (1 if share else 0) + 2 * near)

    beside_copies = []
    if near:
        for spot, side in ((0, 1), (1, total - 1)):
            copy = pltpu.make_async_remote_copy(
                src_ref=refs[count],
                dst_ref=refs[2 * count + 1].at[spot],
                send_sem=scratch[7].at[spot],
                recv_sem=scratch[8].at[spot],
                device_id=(utt, lax.rem(tm + side, total)),
                device_id_type=MESH,
            )
            copy.start()
            beside_copies.append(copy)
    own = [
        pltpu.make_async_copy(blocks[i], outs[i].at[half, second, first], local_sem.at[i])
        for i in range(count)
    ]

    def first_copy(i, step):
        return pltpu.make_async_remote_copy(
            src_ref=blocks[i],
            dst_ref=outs[i].at[half, second, first],
            send_sem=first_send.at[i, step],
            recv_sem=first_recv.at[i, step],
            device_id=(utt, place(lax.rem(first + step, SIDE), second)),
            device_id_type=MESH,
        )

    def ring_copy(i, way, step, order):
        side = 1 - 2 * way
        block = lax.rem(first - order + SIDE, SIDE)
        held, places = ((0, 1), (0, 2), (2, 1), (2, 2))[step] if leap else (step, 1)
        spot = outs[i].at[half, beside(-side * held), block]
        return pltpu.make_async_remote_copy(
            src_ref=blocks[i] if held == 0 and order == 0 else spot,
            dst_ref=spot,
            send_sem=ring_send.at[i, way, step, order],
            recv_sem=ring_recv.at[i, way, step, order],
            device_id=(utt, place(first, beside(side * places))),
            device_id_type=MESH,
        )

    def pair_copy(i, step):
        row = outs[i].at[half, beside(step)]
        return pltpu.make_async_remote_copy(
            src_ref=row,
            dst_ref=row,
            send_sem=pair_send.at[i, step + 3],
            recv_sem=pair_recv.at[i, step + 3],
            device_id=(pair, tm),
            device_id_type=MESH,
        )

    def steps_of(way, order):
        return SIDE // 2 - (order + way) % 2

    for copy in own:
        copy.start()
    for step in ORDER[1:]:
        for i in range(count):
            first_copy(i, step).start()
    for order in ORDER:
        for i in range(count):
            if order > 0:
                first_copy(i, order).wait_recv()
            for way in range(2):
                for step in (0, 1) if leap else (0,):
                    ring_copy(i, way, step, order).start()
    for copy in own:
        copy.wait()
    if share:
        for i in range(count):
            pair_copy(i, 0).start()
    after = {0: (), 1: (2, 3), 2: (), 3: ()} if leap else {0: (1,), 1: (2,), 2: (3,), 3: ()}
    for step in (1, 0, 2, 3) if leap else (0, 1, 2, 3):
        for order in ORDER:
            for i in range(count):
                for way in range(2):
                    if step < steps_of(way, order):
                        ring_copy(i, way, step, order).wait_recv()
                        for later in after[step]:
                            if later < steps_of(way, order):
                                ring_copy(i, way, later, order).start()
        if share:
            for i in range(count):
                pair_copy(i, -step - 1 if step < 3 else 4).start()
                if step < 3:
                    pair_copy(i, step + 1).start()
    for i in range(count):
        for order in ORDER:
            if order > 0:
                first_copy(i, order).wait_send()
            for way in range(2):
                for step in range(steps_of(way, order)):
                    ring_copy(i, way, step, order).wait_send()
    if share:
        for i in range(count):
            for step in range(-3, 5):
                pair_copy(i, step).wait()
    for copy in beside_copies:
        copy.wait()


def gather_blocks(blocks, share, number, space, beside=None):
    count = len(blocks)
    near = 0 if beside is None else 1
    halves = 2 if share else 1
    ring = (count, 2, SIDE // 2, SIDE)
    shapes = [
        jax.ShapeDtypeStruct((halves, SIDE, SIDE) + block.shape, block.dtype) for block in blocks
    ]
    scratch = [
        pltpu.SemaphoreType.DMA((count,)),
        pltpu.SemaphoreType.DMA((count, SIDE)),
        pltpu.SemaphoreType.DMA((count, SIDE)),
        pltpu.SemaphoreType.DMA(ring),
        pltpu.SemaphoreType.DMA(ring),
        pltpu.SemaphoreType.DMA((count, SIDE)),
        pltpu.SemaphoreType.DMA((count, SIDE)),
    ]
    operands = list(blocks)
    if near:
        operands.append(beside)
        shapes.append(jax.ShapeDtypeStruct((2,) + beside.shape, beside.dtype))
        scratch += [pltpu.SemaphoreType.DMA((2,)), pltpu.SemaphoreType.DMA((2,))]
    return pl.pallas_call(
        functools.partial(gather_kernel, count, share, near),
        out_shape=shapes,
        in_specs=[pl.BlockSpec(memory_space=space)] * (count + near),
        out_specs=[pl.BlockSpec(memory_space=space)] * (count + near),
        scratch_shapes=scratch,
        compiler_params=pltpu.CompilerParams(collective_id=number, has_side_effects=True),
        name=f"gather{number}",
    )(*operands)


def exchange_kernel(given, taken, local_sem, send_sem, recv_sem):
    utt = lax.axis_index("utt")
    tm = lax.axis_index("tm")
    groups = given.shape[0]
    barrier = pltpu.get_barrier_semaphore()
    for step in range(1, groups):
        pl.semaphore_signal(
            barrier, inc=1, device_id=(lax.rem(utt + step, groups), tm), device_id_type=MESH
        )
    pl.semaphore_wait(barrier, groups - 1)
    own = pltpu.make_async_copy(given.at[utt], taken.at[utt], local_sem)
    copies = []
    for step in range(1, groups):
        other = lax.rem(utt + step, groups)
        copy = pltpu.make_async_remote_copy(
            src_ref=given.at[other],
            dst_ref=taken.at[utt],
            send_sem=send_sem.at[step],
            recv_sem=recv_sem.at[step],
            device_id=(other, tm),
            device_id_type=MESH,
        )
        copy.start()
        copies.append(copy)
    own.start()
    own.wait()
    for copy in copies:
        copy.wait()


def exchange(windows, number):
    groups = windows.shape[0]
    return pl.pallas_call(
        exchange_kernel,
        out_shape=jax.ShapeDtypeStruct(windows.shape, windows.dtype),
        in_specs=[pl.BlockSpec(memory_space=pltpu.VMEM)],
        out_specs=pl.BlockSpec(memory_space=pltpu.VMEM),
        scratch_shapes=[
            pltpu.SemaphoreType.DMA,
            pltpu.SemaphoreType.DMA((groups,)),
            pltpu.SemaphoreType.DMA((groups,)),
        ],
        compiler_params=pltpu.CompilerParams(collective_id=number, has_side_effects=True),
        name="exchange",
    )(windows)


def utterance_of(indices, bounds):
    return jnp.sum((bounds[None, :] <= indices[:, None]).astype(jnp.int32), axis=1)


def frame_layout(lasting, lengths, ordering):
    phone_total = lasting.shape[0]
    utt_count = lengths.shape[0]
    phone_index = jnp.arange(phone_total, dtype=jnp.int32)
    bounds = jnp.cumsum(lengths)
    utt_first = bounds - lengths
    inclusive = jnp.cumsum(lasting)
    exclusive = inclusive - lasting
    last_frame = jnp.take(inclusive, bounds - 1)
    first_frame = jnp.pad(last_frame, (1, 0))[:utt_count]
    utt_frames = last_frame - first_frame
    slots = jnp.arange(utt_count, dtype=jnp.int32)
    places = jnp.sum(jnp.where(ordering[None, :] == slots[:, None], slots[None, :], 0), axis=1)
    offsets = jnp.sum(jnp.where(places[None, :] < places[:, None], utt_frames[None, :], 0), axis=1)
    moved = offsets - first_frame
    member = (bounds[None, :] > phone_index[:, None]) & (utt_first[None, :] <= phone_index[:, None])
    starting = exclusive + jnp.sum(jnp.where(member, moved[None, :], 0), axis=1)
    return (starting, bounds)


def shards(
    phone_ids,
    durations,
    utt_lengths,
    utt_order,
    buckets,
    embed_table,
    conv1_weight,
    conv2_weight,
    norm_gain,
    mel_weight,
    pre_weight,
    up_weight,
):
    phone_count = phone_ids.shape[1]
    width = embed_table.shape[1]
    device = lax.axis_index("tm")
    core = lax.rem(lax.axis_index("utt"), 2)

    symbols = embed_table.shape[0]
    filters_here = conv1_weight.shape[1]
    part = filters_here // 2
    pick = lambda both: jnp.where(core == 0, both[0], both[1])
    rising = pick(jnp.transpose(up_weight.reshape(up_weight.shape[0], 2, -1), (1, 0, 2)))
    inward = pick(conv1_weight.T.reshape(2, part, -1)).reshape(part * 9, width)
    inward = lax.dot_general(
        inward, embed_table, (((1,), (1,)), ((), ())), preferred_element_type=jnp.float32
    ).astype(BF)
    inward = jnp.pad(inward.reshape(part, 9 * symbols), ((0, 8 - part), (0, 0)))
    outward = jnp.pad(pick(conv2_weight.T.reshape(2, part, -1)), ((0, 8 - part), (0, 0)))
    both = jnp.concatenate([inward, outward], axis=1)
    both, rising, aside = gather_blocks([both, rising], True, 1, pl.ANY, phone_ids)
    both = both.reshape(2 * SIDE * SIDE * 8, -1)
    inward = both[:, : 9 * symbols]
    outward = both[:, 9 * symbols :]

    starting, bounds = frame_layout(durations[0], utt_lengths[0], utt_order[0])
    ending = starting + durations[0]
    nearby = device * phone_count + jnp.arange(-4, phone_count + 4, dtype=jnp.int32)
    phone_labels = jnp.where(nearby < 0, -1, utterance_of(nearby, bounds))
    ids = jnp.concatenate([aside[0, 0, -4:], phone_ids[0], aside[1, 0, :4]])
    table = jnp.arange(symbols, dtype=jnp.int32)[None, :]
    chosen = (phone_ids[0][:, None] == table).astype(BF)
    embedded = jnp.dot(chosen, embed_table, preferred_element_type=jnp.float32)
    center = phone_labels[4 : 4 + phone_count]
    columns = []
    for tap in range(9):
        keep = phone_labels[tap : tap + phone_count] == center
        columns.append((jnp.where(keep, ids[tap : tap + phone_count], -1)[:, None] == table).astype(BF))
    unfolded = jnp.concatenate(columns, axis=1)
    filters = jnp.maximum(
        lax.dot_general(
            unfolded, inward, (((1,), (1,)), ((), ())), preferred_element_type=jnp.float32
        ),
        0.0,
    ).astype(BF)
    conv_out = jnp.dot(filters, outward, preferred_element_type=jnp.float32)
    resid = embedded + conv_out
    middle = jnp.mean(resid, axis=1, keepdims=True)
    spread = jnp.mean((resid - middle) ** 2, axis=1, keepdims=True)
    decoded = ((resid - middle) * lax.rsqrt(spread + EPS) * norm_gain[None, :]).astype(BF)
    mel_width = mel_weight.shape[1]
    mel_ph = jnp.dot(decoded, mel_weight, preferred_element_type=jnp.float32).astype(BF)
    lane = lax.broadcasted_iota(jnp.int32, (phone_count, WIDE), 1)
    told = jnp.where(lane == mel_width, (center + 1).astype(BF)[:, None], jnp.zeros((), BF))
    mel_block = jnp.pad(mel_ph, ((0, 0), (0, WIDE - mel_width))) + told
    (portion,) = gather_blocks([mel_block], False, 2, pltpu.VMEM)
    portion = portion.reshape(-1, WIDE)

    def arranged(values):
        cells = values.reshape(SIDE, SIDE, phone_count)
        return jnp.where(core == 0, jnp.transpose(cells, (1, 0, 2)), cells).reshape(-1)

    groups = lax.axis_size("utt")
    piece = F_DEV // groups
    span = piece + 2 * REACH
    slots = jnp.arange(groups, dtype=jnp.int32)
    source = jnp.sum(
        jnp.where(buckets[0, 0][None, :] == slots[:, None], slots[None, :], 0), axis=1
    )
    frames = (
        device * F_DEV + source[:, None] * piece - REACH
        + jnp.arange(span, dtype=jnp.int32)[None, :]
    ).reshape(-1)
    hit = (frames[:, None] >= arranged(starting)[None, :]) & (
        frames[:, None] < arranged(ending)[None, :]
    )
    windows = jnp.dot(hit.astype(BF), portion, preferred_element_type=jnp.float32).astype(BF)
    arrived = exchange(windows.reshape(groups, span, WIDE), 3)

    out_width = up_weight.shape[2]
    channels = pre_weight.shape[2]
    upsampled = vocoder(
        arrived.reshape(groups * span, WIDE), pre_weight, rising.reshape(2, channels, -1),
        groups, piece, out_width,
    )
    return upsampled.reshape(1, 1, groups, -1, out_width)


def vocoder_kernel(groups, piece, cells_ref, pre, taps_ref, out, taps, total, sem):
    f32 = jnp.float32
    fetch = pltpu.make_async_copy(taps_ref, taps, sem)
    fetch.start()
    cells = cells_ref[...].astype(f32)
    rows = cells.shape[0]
    mel_width, channels = pre.shape[1:]
    width = out.shape[2]

    def ahead(values, steps):
        return values if steps == 0 else pltpu.roll(values, (rows - steps) % rows, 0)

    label = cells[:, mel_width : mel_width + 1]
    summed = jnp.zeros((rows, channels), f32)
    for tap in range(7):
        moved = ahead(cells, tap - 3)
        keep = moved[:, mel_width : mel_width + 1] == label
        kept = jnp.where(keep, moved, 0.0).astype(BF)
        summed += jnp.dot(kept[:, :mel_width], pre[tap], preferred_element_type=f32)
    act = jnp.where(summed >= 0, summed, 0.1 * summed).astype(BF)
    row = lax.broadcasted_iota(jnp.int32, (channels, channels), 0)
    place = lax.broadcasted_iota(jnp.int32, (channels, channels), 1)
    unit = (place // 64) * 8 + ((place // 8) % 8) * 64 + place % 8
    turn = jnp.where(row == unit, 1.0, 0.0).astype(BF)
    turned = jnp.dot(act, turn, preferred_element_type=f32)
    act = act.astype(f32)

    def windowed(values, offset):
        values = ahead(values, REACH + offset)
        if offset != 0:
            same = ahead(cells, REACH + offset) == ahead(cells, REACH)
            keep = jnp.where(same, 1.0, 0.0)[:, mel_width : mel_width + 1]
            values = jnp.where(keep > 0.5, values, 0.0)
        values = values.reshape(groups, rows // groups, channels)[:, :piece]
        return values.reshape(groups * piece, channels).astype(BF)

    late_now = windowed(act, 0)
    early_now = windowed(turned, 0)
    prev = windowed(act, -1)
    nxt = windowed(turned, 1)
    fetch.wait()

    def part(number):
        return taps[number // 8, :, pl.ds(number % 8 * width, width)]

    for r in range(8):
        if r < 4:
            value = jnp.dot(early_now, part(r + 4), preferred_element_type=f32)
            value += jnp.dot(prev, part(r + 12), preferred_element_type=f32)
        else:
            value = jnp.dot(late_now, part(r + 4), preferred_element_type=f32)
            value += jnp.dot(nxt, part(r - 4), preferred_element_type=f32)
        total[:, r, :] = value
    out[...] = total[...].astype(out.dtype)


def vocoder(cells, pre_weight, taps, groups, piece, width):
    vmem = pl.BlockSpec(memory_space=pltpu.VMEM)
    frames = groups * piece
    return pl.pallas_call(
        functools.partial(vocoder_kernel, groups, piece),
        out_shape=jax.ShapeDtypeStruct((frames, 8, width), BF),
        in_specs=[vmem, vmem, pl.BlockSpec(memory_space=pl.ANY)],
        out_specs=vmem,
        scratch_shapes=[
            pltpu.VMEM(taps.shape, taps.dtype),
            pltpu.VMEM((frames, 8, width), jnp.float32),
            pltpu.SemaphoreType.DMA,
        ],
        name="vocoder",
    )(cells, pre_weight, taps)


def solution(mesh):
    placed = (
        P("utt", "tm"),
        P("utt", None),
        P("utt", None),
        P("utt", None),
        P("utt", "tm", None),
        P(),
        P(None, "tm"),
        P(None, "tm"),
        P(),
        P(),
        P(),
        P("tm", None, None),
    )
    return jax.shard_map(
        shards,
        mesh=mesh,
        in_specs=placed,
        out_specs=P("utt", "tm", None, None, None),
        check_vma=False,
    )
```

```python
import functools

import jax
import jax.numpy as jnp
from jax import lax
from jax.experimental import pallas as pl
from jax.experimental.pallas import tpu as pltpu
from jax.sharding import PartitionSpec as P

F_DEV = 256
SIDE = 8
WIDE = 128
REACH = 4
EPS = 1e-05
MESH = pl.DeviceIdType.MESH
BF = jnp.bfloat16


ORDER = (0, 1, 7, 2, 6, 3, 5, 4)


def gather_kernel(count, share, near, *refs):
    blocks = refs[:count]
    outs = refs[count + near : 2 * count + near]
    scratch = refs[2 * (count + near) :]
    local_sem, first_send, first_recv, ring_send, ring_recv, pair_send, pair_recv = scratch[:7]
    total = SIDE * SIDE
    utt = lax.axis_index("utt")
    tm = lax.axis_index("tm")
    core = lax.rem(utt, 2)
    pair = utt + 1 - 2 * core
    y = lax.div(tm, SIDE)
    z = lax.rem(tm, SIDE)
    first = y + core * (z - y)
    second = z + core * (y - z)
    half = core if share else 0

    def place(a, b):
        return a * SIDE + b + core * ((b - a) * SIDE + (a - b))

    def beside(step):
        return lax.rem(second + step + SIDE, SIDE)

    barrier = pltpu.get_barrier_semaphore()

    def greet(step, carry):
        pl.semaphore_signal(
            barrier, inc=1,
            device_id=(utt, place(lax.rem(first + step, SIDE), second)), device_id_type=MESH,
        )
        return carry

    lax.fori_loop(1, SIDE, greet, 0)
    leap = not share
    for side in (1, -1, 2, -2) if leap else (1, -1):
        pl.semaphore_signal(
            barrier, inc=1, device_id=(utt, place(first, beside(side))), device_id_type=MESH
        )
    if share:
        pl.semaphore_signal(barrier, inc=1, device_id=(pair, tm), device_id_type=MESH)
    if near:
        for side in (1, total - 1):
            pl.semaphore_signal(
                barrier, inc=1, device_id=(utt, lax.rem(tm + side, total)), device_id_type=MESH
            )
    pl.semaphore_wait(barrier, SIDE + (1 if share else 3) + (1 if share else 0) + 2 * near)

    beside_copies = []
    if near:
        for spot, side in ((0, 1), (1, total - 1)):
            copy = pltpu.make_async_remote_copy(
                src_ref=refs[count],
                dst_ref=refs[2 * count + 1].at[spot],
                send_sem=scratch[7].at[spot],
                recv_sem=scratch[8].at[spot],
                device_id=(utt, lax.rem(tm + side, total)),
                device_id_type=MESH,
            )
            copy.start()
            beside_copies.append(copy)
    own = [
        pltpu.make_async_copy(blocks[i], outs[i].at[half, second, first], local_sem.at[i])
        for i in range(count)
    ]

    def first_copy(i, step):
        return pltpu.make_async_remote_copy(
            src_ref=blocks[i],
            dst_ref=outs[i].at[half, second, first],
            send_sem=first_send.at[i, step],
            recv_sem=first_recv.at[i, step],
            device_id=(utt, place(lax.rem(first + step, SIDE), second)),
            device_id_type=MESH,
        )

    def ring_copy(i, way, step, order):
        side = 1 - 2 * way
        block = lax.rem(first - order + SIDE, SIDE)
        held, places = ((0, 1), (0, 2), (2, 1), (2, 2))[step] if leap else (step, 1)
        spot = outs[i].at[half, beside(-side * held), block]
        return pltpu.make_async_remote_copy(
            src_ref=blocks[i] if held == 0 and order == 0 else spot,
            dst_ref=spot,
            send_sem=ring_send.at[i, way, step, order],
            recv_sem=ring_recv.at[i, way, step, order],
            device_id=(utt, place(first, beside(side * places))),
            device_id_type=MESH,
        )

    def pair_copy(i, step):
        row = outs[i].at[half, beside(step)]
        return pltpu.make_async_remote_copy(
            src_ref=row,
            dst_ref=row,
            send_sem=pair_send.at[i, step + 3],
            recv_sem=pair_recv.at[i, step + 3],
            device_id=(pair, tm),
            device_id_type=MESH,
        )

    def steps_of(way, order):
        return SIDE // 2 - (order + way) % 2

    for copy in own:
        copy.start()
    for step in ORDER[1:]:
        for i in range(count):
            first_copy(i, step).start()
    for order in ORDER:
        for i in range(count):
            if order > 0:
                first_copy(i, order).wait_recv()
            for way in range(2):
                for step in (1, 0) if leap else (0,):
                    ring_copy(i, way, step, order).start()
    for copy in own:
        copy.wait()
    if share:
        for i in range(count):
            pair_copy(i, 0).start()
    after = {0: (), 1: (3, 2), 2: (), 3: ()} if leap else {0: (1,), 1: (2,), 2: (3,), 3: ()}
    for step in (1, 0, 2, 3) if leap else (0, 1, 2, 3):
        for order in ORDER:
            for i in range(count):
                for way in range(2):
                    if step < steps_of(way, order):
                        ring_copy(i, way, step, order).wait_recv()
                        for later in after[step]:
                            if later < steps_of(way, order):
                                ring_copy(i, way, later, order).start()
        if share:
            for i in range(count):
                pair_copy(i, -step - 1 if step < 3 else 4).start()
                if step < 3:
                    pair_copy(i, step + 1).start()
    for i in range(count):
        for order in ORDER:
            if order > 0:
                first_copy(i, order).wait_send()
            for way in range(2):
                for step in range(steps_of(way, order)):
                    ring_copy(i, way, step, order).wait_send()
    if share:
        for i in range(count):
            for step in range(-3, 5):
                pair_copy(i, step).wait()
    for copy in beside_copies:
        copy.wait()


def gather_blocks(blocks, share, number, space, beside=None):
    count = len(blocks)
    near = 0 if beside is None else 1
    halves = 2 if share else 1
    ring = (count, 2, SIDE // 2, SIDE)
    shapes = [
        jax.ShapeDtypeStruct((halves, SIDE, SIDE) + block.shape, block.dtype) for block in blocks
    ]
    scratch = [
        pltpu.SemaphoreType.DMA((count,)),
        pltpu.SemaphoreType.DMA((count, SIDE)),
        pltpu.SemaphoreType.DMA((count, SIDE)),
        pltpu.SemaphoreType.DMA(ring),
        pltpu.SemaphoreType.DMA(ring),
        pltpu.SemaphoreType.DMA((count, SIDE)),
        pltpu.SemaphoreType.DMA((count, SIDE)),
    ]
    operands = list(blocks)
    if near:
        operands.append(beside)
        shapes.append(jax.ShapeDtypeStruct((2,) + beside.shape, beside.dtype))
        scratch += [pltpu.SemaphoreType.DMA((2,)), pltpu.SemaphoreType.DMA((2,))]
    return pl.pallas_call(
        functools.partial(gather_kernel, count, share, near),
        out_shape=shapes,
        in_specs=[pl.BlockSpec(memory_space=space)] * (count + near),
        out_specs=[pl.BlockSpec(memory_space=space)] * (count + near),
        scratch_shapes=scratch,
        compiler_params=pltpu.CompilerParams(collective_id=number, has_side_effects=True),
        name=f"gather{number}",
    )(*operands)


def exchange_kernel(given, taken, local_sem, send_sem, recv_sem):
    utt = lax.axis_index("utt")
    tm = lax.axis_index("tm")
    groups = given.shape[0]
    barrier = pltpu.get_barrier_semaphore()
    for step in range(1, groups):
        pl.semaphore_signal(
            barrier, inc=1, device_id=(lax.rem(utt + step, groups), tm), device_id_type=MESH
        )
    pl.semaphore_wait(barrier, groups - 1)
    own = pltpu.make_async_copy(given.at[utt], taken.at[utt], local_sem)
    copies = []
    for step in range(1, groups):
        other = lax.rem(utt + step, groups)
        copy = pltpu.make_async_remote_copy(
            src_ref=given.at[other],
            dst_ref=taken.at[utt],
            send_sem=send_sem.at[step],
            recv_sem=recv_sem.at[step],
            device_id=(other, tm),
            device_id_type=MESH,
        )
        copy.start()
        copies.append(copy)
    own.start()
    own.wait()
    for copy in copies:
        copy.wait()


def exchange(windows, number):
    groups = windows.shape[0]
    return pl.pallas_call(
        exchange_kernel,
        out_shape=jax.ShapeDtypeStruct(windows.shape, windows.dtype),
        in_specs=[pl.BlockSpec(memory_space=pltpu.VMEM)],
        out_specs=pl.BlockSpec(memory_space=pltpu.VMEM),
        scratch_shapes=[
            pltpu.SemaphoreType.DMA,
            pltpu.SemaphoreType.DMA((groups,)),
            pltpu.SemaphoreType.DMA((groups,)),
        ],
        compiler_params=pltpu.CompilerParams(collective_id=number, has_side_effects=True),
        name="exchange",
    )(windows)


def utterance_of(indices, bounds):
    return jnp.sum((bounds[None, :] <= indices[:, None]).astype(jnp.int32), axis=1)


def frame_layout(lasting, lengths, ordering):
    phone_total = lasting.shape[0]
    utt_count = lengths.shape[0]
    phone_index = jnp.arange(phone_total, dtype=jnp.int32)
    bounds = jnp.cumsum(lengths)
    utt_first = bounds - lengths
    inclusive = jnp.cumsum(lasting)
    exclusive = inclusive - lasting
    last_frame = jnp.take(inclusive, bounds - 1)
    first_frame = jnp.pad(last_frame, (1, 0))[:utt_count]
    utt_frames = last_frame - first_frame
    slots = jnp.arange(utt_count, dtype=jnp.int32)
    places = jnp.sum(jnp.where(ordering[None, :] == slots[:, None], slots[None, :], 0), axis=1)
    offsets = jnp.sum(jnp.where(places[None, :] < places[:, None], utt_frames[None, :], 0), axis=1)
    moved = offsets - first_frame
    member = (bounds[None, :] > phone_index[:, None]) & (utt_first[None, :] <= phone_index[:, None])
    starting = exclusive + jnp.sum(jnp.where(member, moved[None, :], 0), axis=1)
    return (starting, bounds)


def shards(
    phone_ids,
    durations,
    utt_lengths,
    utt_order,
    buckets,
    embed_table,
    conv1_weight,
    conv2_weight,
    norm_gain,
    mel_weight,
    pre_weight,
    up_weight,
):
    phone_count = phone_ids.shape[1]
    width = embed_table.shape[1]
    device = lax.axis_index("tm")
    core = lax.rem(lax.axis_index("utt"), 2)

    symbols = embed_table.shape[0]
    filters_here = conv1_weight.shape[1]
    part = filters_here // 2
    pick = lambda both: jnp.where(core == 0, both[0], both[1])
    rising = pick(jnp.transpose(up_weight.reshape(up_weight.shape[0], 2, -1), (1, 0, 2)))
    inward = pick(conv1_weight.T.reshape(2, part, -1)).reshape(part * 9, width)
    inward = lax.dot_general(
        inward, embed_table, (((1,), (1,)), ((), ())), preferred_element_type=jnp.float32
    ).astype(BF)
    inward = jnp.pad(inward.reshape(part, 9 * symbols), ((0, 8 - part), (0, 0)))
    outward = jnp.pad(pick(conv2_weight.T.reshape(2, part, -1)), ((0, 8 - part), (0, 0)))
    both = jnp.concatenate([inward, outward], axis=1)
    both, rising, aside = gather_blocks([both, rising], True, 1, pl.ANY, phone_ids)
    both = both.reshape(2 * SIDE * SIDE * 8, -1)
    inward = both[:, : 9 * symbols]
    outward = both[:, 9 * symbols :]

    starting, bounds = frame_layout(durations[0], utt_lengths[0], utt_order[0])
    ending = starting + durations[0]
    nearby = device * phone_count + jnp.arange(-4, phone_count + 4, dtype=jnp.int32)
    phone_labels = jnp.where(nearby < 0, -1, utterance_of(nearby, bounds))
    ids = jnp.concatenate([aside[0, 0, -4:], phone_ids[0], aside[1, 0, :4]])
    table = jnp.arange(symbols, dtype=jnp.int32)[None, :]
    chosen = (phone_ids[0][:, None] == table).astype(BF)
    embedded = jnp.dot(chosen, embed_table, preferred_element_type=jnp.float32)
    center = phone_labels[4 : 4 + phone_count]
    columns = []
    for tap in range(9):
        keep = phone_labels[tap : tap + phone_count] == center
        columns.append((jnp.where(keep, ids[tap : tap + phone_count], -1)[:, None] == table).astype(BF))
    unfolded = jnp.concatenate(columns, axis=1)
    filters = jnp.maximum(
        lax.dot_general(
            unfolded, inward, (((1,), (1,)), ((), ())), preferred_element_type=jnp.float32
        ),
        0.0,
    ).astype(BF)
    conv_out = jnp.dot(filters, outward, preferred_element_type=jnp.float32)
    resid = embedded + conv_out
    middle = jnp.mean(resid, axis=1, keepdims=True)
    spread = jnp.mean((resid - middle) ** 2, axis=1, keepdims=True)
    decoded = ((resid - middle) * lax.rsqrt(spread + EPS) * norm_gain[None, :]).astype(BF)
    mel_width = mel_weight.shape[1]
    mel_ph = jnp.dot(decoded, mel_weight, preferred_element_type=jnp.float32).astype(BF)
    lane = lax.broadcasted_iota(jnp.int32, (phone_count, WIDE), 1)
    told = jnp.where(lane == mel_width, (center + 1).astype(BF)[:, None], jnp.zeros((), BF))
    mel_block = jnp.pad(mel_ph, ((0, 0), (0, WIDE - mel_width))) + told
    (portion,) = gather_blocks([mel_block], False, 2, pltpu.VMEM)
    portion = portion.reshape(-1, WIDE)

    def arranged(values):
        cells = values.reshape(SIDE, SIDE, phone_count)
        return jnp.where(core == 0, jnp.transpose(cells, (1, 0, 2)), cells).reshape(-1)

    groups = lax.axis_size("utt")
    piece = F_DEV // groups
    span = piece + 2 * REACH
    slots = jnp.arange(groups, dtype=jnp.int32)
    source = jnp.sum(
        jnp.where(buckets[0, 0][None, :] == slots[:, None], slots[None, :], 0), axis=1
    )
    frames = (
        device * F_DEV + source[:, None] * piece - REACH
        + jnp.arange(span, dtype=jnp.int32)[None, :]
    ).reshape(-1)
    hit = (frames[:, None] >= arranged(starting)[None, :]) & (
        frames[:, None] < arranged(ending)[None, :]
    )
    windows = jnp.dot(hit.astype(BF), portion, preferred_element_type=jnp.float32).astype(BF)
    arrived = exchange(windows.reshape(groups, span, WIDE), 3)

    out_width = up_weight.shape[2]
    channels = pre_weight.shape[2]
    upsampled = vocoder(
        arrived.reshape(groups * span, WIDE), pre_weight, rising.reshape(2, channels, -1),
        groups, piece, out_width,
    )
    return upsampled.reshape(1, 1, groups, -1, out_width)


def vocoder_kernel(groups, piece, cells_ref, pre, taps_ref, out, taps, total, sem):
    f32 = jnp.float32
    fetch = pltpu.make_async_copy(taps_ref, taps, sem)
    fetch.start()
    cells = cells_ref[...].astype(f32)
    rows = cells.shape[0]
    mel_width, channels = pre.shape[1:]
    width = out.shape[2]

    def ahead(values, steps):
        return values if steps == 0 else pltpu.roll(values, (rows - steps) % rows, 0)

    label = cells[:, mel_width : mel_width + 1]
    summed = jnp.zeros((rows, channels), f32)
    for tap in range(7):
        moved = ahead(cells, tap - 3)
        keep = moved[:, mel_width : mel_width + 1] == label
        kept = jnp.where(keep, moved, 0.0).astype(BF)
        summed += jnp.dot(kept[:, :mel_width], pre[tap], preferred_element_type=f32)
    act = jnp.where(summed >= 0, summed, 0.1 * summed).astype(BF)
    row = lax.broadcasted_iota(jnp.int32, (channels, channels), 0)
    place = lax.broadcasted_iota(jnp.int32, (channels, channels), 1)
    unit = (place // 64) * 8 + ((place // 8) % 8) * 64 + place % 8
    turn = jnp.where(row == unit, 1.0, 0.0).astype(BF)
    turned = jnp.dot(act, turn, preferred_element_type=f32)
    act = act.astype(f32)

    def windowed(values, offset):
        values = ahead(values, REACH + offset)
        if offset != 0:
            same = ahead(cells, REACH + offset) == ahead(cells, REACH)
            keep = jnp.where(same, 1.0, 0.0)[:, mel_width : mel_width + 1]
            values = jnp.where(keep > 0.5, values, 0.0)
        values = values.reshape(groups, rows // groups, channels)[:, :piece]
        return values.reshape(groups * piece, channels).astype(BF)

    late_now = windowed(act, 0)
    early_now = windowed(turned, 0)
    prev = windowed(act, -1)
    nxt = windowed(turned, 1)
    fetch.wait()

    def part(number):
        return taps[number // 8, :, pl.ds(number % 8 * width, width)]

    for r in range(8):
        if r < 4:
            value = jnp.dot(early_now, part(r + 4), preferred_element_type=f32)
            value += jnp.dot(prev, part(r + 12), preferred_element_type=f32)
        else:
            value = jnp.dot(late_now, part(r + 4), preferred_element_type=f32)
            value += jnp.dot(nxt, part(r - 4), preferred_element_type=f32)
        total[:, r, :] = value
    out[...] = total[...].astype(out.dtype)


def vocoder(cells, pre_weight, taps, groups, piece, width):
    vmem = pl.BlockSpec(memory_space=pltpu.VMEM)
    frames = groups * piece
    return pl.pallas_call(
        functools.partial(vocoder_kernel, groups, piece),
        out_shape=jax.ShapeDtypeStruct((frames, 8, width), BF),
        in_specs=[vmem, vmem, pl.BlockSpec(memory_space=pl.ANY)],
        out_specs=vmem,
        scratch_shapes=[
            pltpu.VMEM(taps.shape, taps.dtype),
            pltpu.VMEM((frames, 8, width), jnp.float32),
            pltpu.SemaphoreType.DMA,
        ],
        name="vocoder",
    )(cells, pre_weight, taps)


def solution(mesh):
    placed = (
        P("utt", "tm"),
        P("utt", None),
        P("utt", None),
        P("utt", None),
        P("utt", "tm", None),
        P(),
        P(None, "tm"),
        P(None, "tm"),
        P(),
        P(),
        P(),
        P("tm", None, None),
    )
    return jax.shard_map(
        shards,
        mesh=mesh,
        in_specs=placed,
        out_specs=P("utt", "tm", None, None, None),
        check_vma=False,
    )
```
